32 devices in a mesh: groups: 2 (over x), blk: 16 (over z, y, core).
Axes of the slice: x: 2, y: 2, z: 4, core: 2. Of those that a mesh axis runs over, the one named last changes fastest.
Arguments:
- queries: bfloat16 [32, 8192], P(('groups', 'blk')), parts along dimension 0, may hold values from -100 to 100
- prefix_key_value: bfloat16 [2, 32768, 1024], P(None, ('groups', 'blk')), parts along dimension 1, may hold values from -7 to 7
- suffix_key_value: bfloat16 [32, 2, 512, 1024], P(('groups', 'blk')), parts along dimension 0, may hold values from -9 to 9
- fresh_key_value: bfloat16 [32, 2, 1024], P(('groups', 'blk')), parts along dimension 0, may hold values from -9 to 9
- lengths: int32 [32], P('groups'), parts along dimension 0, may hold values from 1 to 512, 4096 in all
- home: int32 [32], P('groups'), parts along dimension 0, may hold values from 0 to 15, each once
Outputs:
- attended: bfloat16 [32, 8192], P(('groups', 'blk')), parts along dimension 0
The draws below stay inside these ranges and needn't reach their ends.
There are 2 independent parts, one for each index of `groups`. The reference program is written for one: setup_inputs(seed, part) draws one part's arguments, and reference() takes and returns one part's arrays. A program takes and returns all parts, laid end to end along the dimension named above; each array names one. Nothing has to cross between parts.
Inputs may be any that keep to these rules, and one draw needn't show every extreme that they name: Row r's suffix cache lies in slot home[r]; every slot holds exactly one row. `lengths`: some row has exactly 512 suffix tokens.
All inputs are finite; a program needn't handle non-finite values.
Results may differ from the reference program's by a relative error of at most 0.0049.
Values may be sent and summed in bfloat16 or wider, within the bound.
No kernel may reach another device: no remote copies, remote signals or barrier semaphores. Data moves between devices by JAX's collectives and lax.ppermute only.
A program may use at most 128 MiB of HBM per device.

```python
import math
import jax
import jax.numpy as jnp
import numpy as np
from jax import lax

QUERY_HEADS = 64
KEY_VALUE_HEADS = 8
HEAD_WIDTH = 128
ROWS_DEV = 1
PREFIX_PER_BLOCK = 1024
SUFFIX_SLOTS = 512
REVISION_ROWS = 16
PREFIX_TOTAL = 16384
N_BLK = 16


def prefix_stream(random_seed_key):
    table_entries = jax.random.normal(jax.random.fold_in(random_seed_key, 11), (2, PREFIX_TOTAL, KEY_VALUE_HEADS * HEAD_WIDTH), jnp.float32)
    table_entries = jnp.clip(table_entries, -6.0, 6.0)
    return table_entries


def draw_prefix_key_value(key, part):
    table_entries = prefix_stream(key)
    return table_entries.astype(jnp.bfloat16)


def draw_queries(key, part):
    base = 3.0 * jax.random.normal(jax.random.fold_in(key, 21), (REVISION_ROWS, QUERY_HEADS * HEAD_WIDTH), jnp.float32)
    base = jnp.clip(base, -100.0, 100.0)
    return base.astype(jnp.bfloat16)


def level_of(own_key, dims, cuts, least, high):
    factor_of = 1.0
    for position, blocks in cuts:
        steps = jax.random.uniform(jax.random.fold_in(jax.random.fold_in(own_key, 6), position), (blocks,), jnp.float32, least / len(cuts), high / len(cuts))
        factor_of = factor_of * jnp.repeat(jnp.exp(steps), dims[position] // blocks).reshape((-1,) + (1,) * (len(dims) - 1 - position))
    return factor_of


def split_up(number_of, total, bound, skew):
    portions = [(1 << 20) // math.isqrt(standing ** skew) + 1 for standing in range(2, number_of + 1)]
    rest, given = total - bound - (number_of - 1), [1] * (number_of - 1)
    while rest > 0:
        free = [i for i in range(number_of - 1) if given[i] < bound]
        whole, remaining = sum([portions[i] for i in free]), rest
        for i in free:
            extra = min(bound - given[i], max(1, remaining * portions[i] // whole), rest)
            given[i] = given[i] + extra
            rest = rest - extra
    return np.array([bound] + given)


def uneven_parts(rng, count, total, bound, lean):
    if count == 2:
        one = jax.random.randint(rng, (), max(1, total - bound), min(bound, total - 1) + 1)
        return jnp.stack([one, total - one])
    sizes = jnp.asarray(split_up(count, total, bound, lean), jnp.int32)
    couples = (count - 1) // 2
    giver, taker = sizes[1:1 + 2 * couples:2], sizes[2:2 + 2 * couples:2]
    margin = jnp.minimum(giver - 1, bound - taker)
    shifted = jax.random.randint(jax.random.fold_in(rng, 1), (couples,), 0, 1 << 20) % (margin + 1)
    sizes = sizes.at[1:1 + 2 * couples:2].set(giver - shifted).at[2:2 + 2 * couples:2].set(taker + shifted)
    return sizes[jax.random.permutation(jax.random.fold_in(rng, 2), count)]


def centred(rng, extent, spread, bound, split=(), held_as=jnp.bfloat16):
    level = level_of(rng, extent, split, -0.22, 0.18) if split else 1.0
    values = jax.random.normal(rng, extent, jnp.float32) * spread * level
    return jnp.minimum(jnp.maximum(values, -bound), bound).astype(held_as)


def setup_inputs(seed: int = 0, part: int = 0) -> dict:
    seeds = jax.random.split(jax.random.key(seed), 7)
    own_keys = jax.random.split(jax.random.fold_in(seeds[6], part), 7)
    queries = draw_queries(jax.random.fold_in(jax.random.fold_in(seeds[6], part), 71), part)
    prefix_key_value = draw_prefix_key_value(jax.random.fold_in(jax.random.fold_in(seeds[6], part), 71), part)
    suffix_key_value = centred(own_keys[2], (REVISION_ROWS, 2, SUFFIX_SLOTS, KEY_VALUE_HEADS * HEAD_WIDTH), 1.5, 9.0, ((0, 16),))
    fresh_key_value = centred(own_keys[3], (REVISION_ROWS, 2, KEY_VALUE_HEADS * HEAD_WIDTH), 1.5, 9.0, ((0, 16),))
    lengths = uneven_parts(own_keys[4], REVISION_ROWS, REVISION_ROWS * SUFFIX_SLOTS // 2, SUFFIX_SLOTS, 2).astype(jnp.int32)
    home = jax.random.permutation(own_keys[5], REVISION_ROWS).astype(jnp.int32)
    return {"queries": queries, "prefix_key_value": prefix_key_value, "suffix_key_value": suffix_key_value, "fresh_key_value": fresh_key_value, "lengths": lengths, "home": home}


def part_stats(scores, values):
    peak = jnp.max(scores, axis=-1)
    exponent = jnp.exp(scores - peak[..., None])
    totals = jnp.sum(exponent, axis=-1)
    weights = exponent.astype(jnp.bfloat16).astype(jnp.float32)
    accum = jnp.einsum("rhgt,rthd->rhgd", weights, values)
    return peak, totals, accum


def reference(queries, prefix_key_value, suffix_key_value, fresh_key_value, lengths, home):
    query_group = QUERY_HEADS // KEY_VALUE_HEADS
    score_scale = HEAD_WIDTH ** -0.5
    query_head_rows = queries.reshape(REVISION_ROWS, KEY_VALUE_HEADS, query_group, HEAD_WIDTH).astype(jnp.float32)

    def suffix_row(item):
        query_row, slot_id, length = item
        cache_tile_index = lax.dynamic_index_in_dim(suffix_key_value, slot_id, 0, keepdims=False)
        row_key_slice = cache_tile_index[0].reshape(SUFFIX_SLOTS, KEY_VALUE_HEADS, HEAD_WIDTH).astype(jnp.float32)
        row_value_slice = cache_tile_index[1].reshape(SUFFIX_SLOTS, KEY_VALUE_HEADS, HEAD_WIDTH).astype(jnp.float32)
        scores = jnp.einsum("hgd,thd->hgt", query_row, row_key_slice) * score_scale
        live_mask = jnp.arange(SUFFIX_SLOTS, dtype=jnp.int32) < length
        scores = jnp.where(live_mask[None, None, :], scores, -jnp.inf)
        peak, totals, accum = part_stats(scores[None], row_value_slice[None])
        return peak[0], totals[0], accum[0]

    suffix_score_peak, suffix_weight_sum, suffix_accum_sum = lax.map(suffix_row, (query_head_rows, home, lengths))
    fresh_token_keys = fresh_key_value[:, 0].reshape(REVISION_ROWS, KEY_VALUE_HEADS, HEAD_WIDTH).astype(jnp.float32)
    fresh_token_values = fresh_key_value[:, 1].reshape(REVISION_ROWS, KEY_VALUE_HEADS, HEAD_WIDTH).astype(jnp.float32)
    new_peak = jnp.einsum("rhgd,rhd->rhg", query_head_rows, fresh_token_keys) * score_scale
    new_total = jnp.ones_like(new_peak)
    fresh_token_accum = jnp.broadcast_to(fresh_token_values[:, :, None, :], (REVISION_ROWS, KEY_VALUE_HEADS, query_group, HEAD_WIDTH))
    row_ids = jnp.arange(REVISION_ROWS, dtype=jnp.int32)

    def block_step(carry, block_id):
        run_peak, run_num, run_den = carry
        start_offset = (block_id * PREFIX_PER_BLOCK).astype(jnp.int32)
        cache_tile_index = lax.dynamic_slice_in_dim(prefix_key_value, start_offset, PREFIX_PER_BLOCK, 1)
        block_key_rows = cache_tile_index[0].reshape(PREFIX_PER_BLOCK, KEY_VALUE_HEADS, HEAD_WIDTH).astype(jnp.float32)
        block_value_rows = cache_tile_index[1].reshape(PREFIX_PER_BLOCK, KEY_VALUE_HEADS, HEAD_WIDTH).astype(jnp.float32)
        scores = jnp.einsum("rhgd,thd->rhgt", query_head_rows, block_key_rows) * score_scale
        prefix_score_peak = jnp.max(scores, axis=-1)
        exponent = jnp.exp(scores - prefix_score_peak[..., None])
        prefix_weight_sum = jnp.sum(exponent, axis=-1)
        weights = exponent.astype(jnp.bfloat16).astype(jnp.float32)
        prefix_accum_sum = jnp.einsum("rhgt,thd->rhgd", weights, block_value_rows)
        suf_here = (home // ROWS_DEV == block_id)[:, None, None]
        new_here = (row_ids // ROWS_DEV == block_id)[:, None, None]
        suf_peak_b = jnp.where(suf_here, suffix_score_peak, -jnp.inf)
        new_peak_b = jnp.where(new_here, new_peak, -jnp.inf)
        peak = jnp.maximum(prefix_score_peak, jnp.maximum(suf_peak_b, new_peak_b))
        pre_fac = jnp.exp(prefix_score_peak - peak)
        suf_fac = jnp.where(suf_here, jnp.exp(suf_peak_b - peak), 0.0)
        new_fac = jnp.where(new_here, jnp.exp(new_peak_b - peak), 0.0)
        totals = pre_fac * prefix_weight_sum + suf_fac * suffix_weight_sum + new_fac * new_total
        accum = pre_fac[..., None] * prefix_accum_sum + suf_fac[..., None] * suffix_accum_sum + new_fac[..., None] * fresh_token_accum
        normed = (accum / totals[..., None]).astype(jnp.bfloat16)
        normed = lax.optimization_barrier(normed).astype(jnp.float32)
        lse = peak + jnp.log(totals)
        next_peak = jnp.maximum(run_peak, lse)
        old_fac = jnp.exp(run_peak - next_peak)
        blk_fac = jnp.exp(lse - next_peak)
        run_num = run_num * old_fac[..., None] + blk_fac[..., None] * normed
        run_den = run_den * old_fac + blk_fac
        return (next_peak, run_num, run_den), None

    initial_carry = (jnp.full((REVISION_ROWS, KEY_VALUE_HEADS, query_group), -jnp.inf, jnp.float32),
                   jnp.zeros((REVISION_ROWS, KEY_VALUE_HEADS, query_group, HEAD_WIDTH), jnp.float32),
                   jnp.zeros((REVISION_ROWS, KEY_VALUE_HEADS, query_group), jnp.float32))
    final, _ = lax.scan(block_step, initial_carry, jnp.arange(N_BLK, dtype=jnp.int32))
    result = final[1] / final[2][..., None]
    return result.reshape(REVISION_ROWS, QUERY_HEADS * HEAD_WIDTH).astype(jnp.bfloat16)
```

```python
import functools
import math

import jax
import jax.numpy as jnp
from jax import lax
from jax.experimental import pallas as pl
from jax.experimental.pallas import tpu as pltpu
from jax.sharding import PartitionSpec as P

QUERY_HEADS = 64
KEY_VALUE_HEADS = 8
HEAD_WIDTH = 128
LANES = 128

OUT_WIDTH = QUERY_HEADS * HEAD_WIDTH
PACK_WIDTH = OUT_WIDTH + 2 * LANES

SCORE_SCALE = HEAD_WIDTH ** (-0.5)
EXP2_SCALE = SCORE_SCALE * math.log2(math.e)


def pack_lse(lse):
    lane = lax.broadcasted_iota(jnp.int32, lse.shape, 1)
    high = lse.astype(jnp.bfloat16)
    rest = lse - high.astype(jnp.float32)
    middle = rest.astype(jnp.bfloat16)
    low = (rest - middle.astype(jnp.float32)).astype(jnp.bfloat16)
    first = jnp.where(lane < QUERY_HEADS, high.astype(jnp.float32), middle.astype(jnp.float32))
    return first.astype(jnp.bfloat16), low


def unpack_lse(first, low):
    first = first.astype(jnp.float32)
    return first + pltpu.roll(first, QUERY_HEADS, 1) + low.astype(jnp.float32)


def slot_of_row(distance, bits):
    slot = 0
    for i in range(bits):
        slot = slot + (lax.shift_right_logical(distance, bits - 1 - i) & 1) * (1 << i)
    return slot


def attend_kernel(
    home_ref,
    lengths_ref,
    query_ref,
    fresh_ref,
    prefix_ref,
    suffix_ref,
    keep_ref,
    keep_lse_ref,
    send_ref,
    prefix_buf,
    suffix_buf,
    query_buf,
    prefix_sem,
    suffix_sem,
    *,
    slots,
):
    bits = slots.bit_length() - 1
    half = slots // 2
    group = QUERY_HEADS // KEY_VALUE_HEADS
    pack = max(1, min(group, LANES // slots))
    steps = QUERY_HEADS // pack
    rows = pack * slots
    suffix_length = suffix_ref.shape[2]

    def head_copies(head):
        columns = pl.ds(head * HEAD_WIDTH, HEAD_WIDTH)
        return (
            pltpu.make_async_copy(
                prefix_ref.at[:, :, columns], prefix_buf.at[:, :, columns], prefix_sem.at[head]
            ),
            pltpu.make_async_copy(
                suffix_ref.at[0, :, :, columns], suffix_buf.at[:, :, columns], suffix_sem.at[head]
            ),
        )

    for head in range(KEY_VALUE_HEADS):
        for copy in head_copies(head):
            copy.start()

    me = lax.axis_index("blk")

    def find(row, found):
        return jnp.where(home_ref[row] == me, row, found)

    suffix_row = lax.fori_loop(0, slots, find, 0, unroll=slots <= 16)
    suffix_slot = slot_of_row(me ^ suffix_row, bits)
    live = lengths_ref[suffix_row]

    query_buf[...] = query_ref[...].astype(jnp.float32)
    suffix_query = query_buf[pl.ds(suffix_slot, 1), :]
    own_query = query_buf[0:1, :]

    slot_ids = lax.broadcasted_iota(jnp.int32, (pack, slots, 1), 1).reshape(rows, 1)
    is_suffix = slot_ids == suffix_slot
    is_own = slot_ids == 0
    live_mask = lax.broadcasted_iota(jnp.int32, (1, suffix_length), 1) < live
    lane = lax.broadcasted_iota(jnp.int32, (slots, LANES), 1) & (QUERY_HEADS - 1)

    def spread(values):
        width = values.shape[-1]
        return jnp.broadcast_to(values[:, None, :], (pack, slots, width)).reshape(rows, width)

    def contract(left, right):
        return lax.dot_general(
            left, right, (((1,), (1,)), ((), ())), preferred_element_type=jnp.float32
        )

    lse_all = jnp.zeros((slots, LANES), jnp.float32)
    for step in range(steps):
        head = step * pack // group
        if step * pack % group == 0:
            for copy in head_copies(head):
                copy.wait()
        columns = slice(head * HEAD_WIDTH, (head + 1) * HEAD_WIDTH)
        heads = [step * pack + i for i in range(pack)]

        def chunk(array, c):
            return array[:, c * HEAD_WIDTH : (c + 1) * HEAD_WIDTH]

        queries = jnp.concatenate([chunk(query_ref, c) for c in heads], axis=0)
        scores = contract(queries, prefix_buf[0, :, columns])
        peak = jnp.max(scores, axis=1, keepdims=True)
        weights = jnp.exp2((scores - peak) * EXP2_SCALE)
        total = jnp.sum(weights, axis=1, keepdims=True)
        accum = jnp.dot(
            weights.astype(jnp.bfloat16),
            prefix_buf[1, :, columns],
            preferred_element_type=jnp.float32,
        )

        slot_query = jnp.concatenate([chunk(suffix_query, c) for c in heads], axis=0)
        slot_scores = contract(slot_query.astype(jnp.bfloat16), suffix_buf[0, :, columns])
        slot_scores = jnp.where(live_mask, slot_scores, -jnp.inf)
        slot_peak = jnp.max(slot_scores, axis=1, keepdims=True)
        slot_weights = jnp.exp2((slot_scores - slot_peak) * EXP2_SCALE)
        slot_total = jnp.sum(slot_weights, axis=1, keepdims=True)
        slot_accum = jnp.dot(
            slot_weights.astype(jnp.bfloat16),
            suffix_buf[1, :, columns],
            preferred_element_type=jnp.float32,
        )

        new_query = jnp.concatenate([chunk(own_query, c) for c in heads], axis=0)
        new_key = fresh_ref[0, 0:1, columns].astype(jnp.float32)
        new_value = fresh_ref[0, 1:2, columns].astype(jnp.float32)
        new_peak = jnp.sum(new_query * new_key, axis=1, keepdims=True)

        slot_peak = jnp.where(is_suffix, spread(slot_peak), -jnp.inf)
        new_peak = jnp.where(is_own, spread(new_peak), -jnp.inf)
        highest = jnp.maximum(peak, jnp.maximum(slot_peak, new_peak))
        factor = jnp.exp2((peak - highest) * EXP2_SCALE)
        slot_factor = jnp.exp2((slot_peak - highest) * EXP2_SCALE)
        new_factor = jnp.exp2((new_peak - highest) * EXP2_SCALE)
        total = factor * total + slot_factor * spread(slot_total) + new_factor
        accum = factor * accum + slot_factor * spread(slot_accum) + new_factor * new_value
        normed = accum / total
        lse = highest * SCORE_SCALE + jnp.log(total)
        for i, c in enumerate(heads):
            out = normed[i * slots : (i + 1) * slots]
            keep_ref[:, c * HEAD_WIDTH : (c + 1) * HEAD_WIDTH] = out[:half]
            send_ref[:, c * HEAD_WIDTH : (c + 1) * HEAD_WIDTH] = out[half:].astype(jnp.bfloat16)
            lse_all = jnp.where(lane == c, lse[i * slots : (i + 1) * slots], lse_all)
    keep_lse_ref[...] = lse_all[:half]
    first, low = pack_lse(lse_all[half:])
    send_ref[:, OUT_WIDTH : OUT_WIDTH + LANES] = first
    send_ref[:, OUT_WIDTH + LANES : PACK_WIDTH] = low


def merge_kernel(keep_ref, keep_lse_ref, landed_ref, *out_refs, rows):
    lse_keep = keep_lse_ref[...]
    lse_landed = unpack_lse(
        landed_ref[:, OUT_WIDTH : OUT_WIDTH + LANES], landed_ref[:, OUT_WIDTH + LANES : PACK_WIDTH]
    )
    highest = jnp.maximum(lse_keep, lse_landed)
    weight_keep = jnp.exp(lse_keep - highest)
    weight_landed = jnp.exp(lse_landed - highest)
    total = weight_keep + weight_landed
    weight_keep = weight_keep / total
    weight_landed = weight_landed / total
    half = rows // 2
    for c in range(QUERY_HEADS):
        columns = slice(c * HEAD_WIDTH, (c + 1) * HEAD_WIDTH)
        merged = weight_keep[:, c : c + 1] * keep_ref[:, columns] + weight_landed[
            :, c : c + 1
        ] * landed_ref[:, columns].astype(jnp.float32)
        if half:
            out_refs[0][:, columns] = merged[:half]
            out_refs[2][:, columns] = merged[half:].astype(jnp.bfloat16)
        else:
            out_refs[0][:, columns] = merged.astype(jnp.bfloat16)
    if half:
        lse = highest + jnp.log(total)
        out_refs[1][...] = lse[:half]
        first, low = pack_lse(lse[half:])
        out_refs[2][:, OUT_WIDTH : OUT_WIDTH + LANES] = first
        out_refs[2][:, OUT_WIDTH + LANES : PACK_WIDTH] = low


def partial_shapes(rows):
    return (
        jax.ShapeDtypeStruct((rows, OUT_WIDTH), jnp.float32),
        jax.ShapeDtypeStruct((rows, LANES), jnp.float32),
        jax.ShapeDtypeStruct((rows, PACK_WIDTH), jnp.bfloat16),
    )


def per_device(queries, prefix_key_value, suffix_key_value, fresh_key_value, lengths, home):
    slots = lax.axis_size("blk")
    bits = slots.bit_length() - 1
    assert queries.shape[0] == 1 and slots == 1 << bits and slots > 1
    vmem = pl.BlockSpec(memory_space=pltpu.VMEM)
    smem = pl.BlockSpec(memory_space=pltpu.SMEM)
    hbm = pl.BlockSpec(memory_space=pl.ANY)

    def swap(array, step):
        return lax.ppermute(array, "blk", [(i, i ^ step) for i in range(slots)])

    gathered = queries
    for i in range(bits):
        gathered = jnp.concatenate([gathered, swap(gathered, slots >> (i + 1))], axis=0)

    half = slots // 2
    prefix_length = prefix_key_value.shape[1]
    suffix_length = suffix_key_value.shape[2]
    width = KEY_VALUE_HEADS * HEAD_WIDTH
    keep, keep_lse, send = pl.pallas_call(
        functools.partial(attend_kernel, slots=slots),
        out_shape=partial_shapes(half),
        in_specs=[smem, smem, vmem, vmem, hbm, hbm],
        out_specs=(vmem, vmem, vmem),
        scratch_shapes=[
            pltpu.VMEM((2, prefix_length, width), jnp.bfloat16),
            pltpu.VMEM((2, suffix_length, width), jnp.bfloat16),
            pltpu.VMEM((slots, OUT_WIDTH), jnp.float32),
            pltpu.SemaphoreType.DMA((KEY_VALUE_HEADS,)),
            pltpu.SemaphoreType.DMA((KEY_VALUE_HEADS,)),
        ],
        compiler_params=pltpu.CompilerParams(vmem_limit_bytes=40 * 1024 * 1024),
        name="attend",
    )(home, lengths, gathered, fresh_key_value, prefix_key_value, suffix_key_value)

    for i in range(bits):
        rows = half >> i
        landed = swap(send, 1 << i)
        if rows > 1:
            shapes = partial_shapes(rows // 2)
        else:
            shapes = (jax.ShapeDtypeStruct((1, OUT_WIDTH), jnp.bfloat16),)
        merged = pl.pallas_call(
            functools.partial(merge_kernel, rows=rows),
            out_shape=shapes,
            in_specs=[vmem, vmem, vmem],
            out_specs=(vmem,) * len(shapes),
            compiler_params=pltpu.CompilerParams(vmem_limit_bytes=16 * 1024 * 1024),
            name="merge",
        )(keep, keep_lse, landed)
        if rows > 1:
            keep, keep_lse, send = merged
    return merged[0]


def solution(mesh):
    placed = (
        P(("groups", "blk"), None),
        P(None, ("groups", "blk"), None),
        P(("groups", "blk"), None, None, None),
        P(("groups", "blk"), None, None),
        P("groups"),
        P("groups"),
    )
    return jax.shard_map(
        per_device,
        mesh=mesh,
        in_specs=placed,
        out_specs=P(("groups", "blk"), None),
        check_vma=False,
    )
```

```python
import functools
import math

import jax
import jax.numpy as jnp
from jax import lax
from jax.experimental import pallas as pl
from jax.experimental.pallas import tpu as pltpu
from jax.sharding import PartitionSpec as P

QUERY_HEADS = 64
KEY_VALUE_HEADS = 8
HEAD_WIDTH = 128
LANES = 128

OUT_WIDTH = QUERY_HEADS * HEAD_WIDTH
PACK_WIDTH = OUT_WIDTH + 2 * LANES

SCORE_SCALE = HEAD_WIDTH ** (-0.5)
EXP2_SCALE = SCORE_SCALE * math.log2(math.e)

PREFETCH_VMEM = 16 * 1024 * 1024
MERGE_VMEM = 16 * 1024 * 1024
ATTEND_VMEM = 24 * 1024 * 1024


def pack_lse(lse):
    lane = lax.broadcasted_iota(jnp.int32, lse.shape, 1)
    high = lse.astype(jnp.bfloat16)
    rest = lse - high.astype(jnp.float32)
    middle = rest.astype(jnp.bfloat16)
    low = (rest - middle.astype(jnp.float32)).astype(jnp.bfloat16)
    first = jnp.where(lane < QUERY_HEADS, high.astype(jnp.float32), middle.astype(jnp.float32))
    return first.astype(jnp.bfloat16), low


def unpack_lse(first, low):
    first = first.astype(jnp.float32)
    return first + pltpu.roll(first, QUERY_HEADS, 1) + low.astype(jnp.float32)


def slot_of_row(distance, bits):
    slot = 0
    for i in range(bits):
        slot = slot + (lax.shift_right_logical(distance, bits - 1 - i) & 1) * (1 << i)
    return slot


def prefetch_kernel(
    home_ref, lengths_ref, query_hbm, fresh_hbm, prefix_hbm, suffix_hbm,
    query_ref, fresh_ref, key_ref, value_ref, suffix_ref, live_ref, sems, *, slots
):
    copies = [
        pltpu.make_async_copy(query_hbm, query_ref, sems.at[0]),
        pltpu.make_async_copy(fresh_hbm, fresh_ref, sems.at[1]),
    ]
    pieces = KEY_VALUE_HEADS
    for source, target in (
        (prefix_hbm.at[0], key_ref),
        (prefix_hbm.at[1], value_ref),
        (suffix_hbm.at[0], suffix_ref.at[0]),
        (suffix_hbm.at[1], suffix_ref.at[1]),
    ):
        rows = target.shape[0] // pieces
        for piece in range(pieces):
            span = pl.ds(piece * rows, rows)
            copies.append(
                pltpu.make_async_copy(source.at[span], target.at[span], sems.at[len(copies)])
            )
    for copy in copies:
        copy.start()
    me = lax.axis_index("blk")

    def find(row, found):
        return jnp.where(home_ref[row] == me, row, found)

    suffix_row = lax.fori_loop(0, slots, find, 0, unroll=slots <= 16)
    bits = slots.bit_length() - 1
    lane = lax.broadcasted_iota(jnp.int32, live_ref.shape, 1)
    live_ref[...] = jnp.where(
        lane == 0, slot_of_row(me ^ suffix_row, bits), lengths_ref[suffix_row]
    )
    for copy in copies:
        copy.wait()


def join_kernel(first_ref, second_ref, out_ref):
    rows = first_ref.shape[0]
    out_ref[:rows] = first_ref[...]
    out_ref[rows:] = second_ref[...]


def attend_kernel(
    live_ref,
    query_ref,
    fresh_ref,
    key_ref,
    value_ref,
    suffix_ref,
    keep_ref,
    keep_lse_ref,
    send_ref,
    *,
    slots,
):
    half = slots // 2
    group = QUERY_HEADS // KEY_VALUE_HEADS
    pack = max(1, min(group, LANES // slots))
    steps = QUERY_HEADS // pack
    rows = pack * slots
    suffix_length = suffix_ref.shape[1]

    suffix_slot = live_ref[:, 0:1]
    live = live_ref[:, 1:2]

    all_rows = lax.broadcasted_iota(jnp.int32, (slots, 1), 0)
    own_query = query_ref[...].astype(jnp.float32)
    suffix_query = jnp.sum(
        jnp.where(all_rows == suffix_slot, own_query, 0.0), axis=0, keepdims=True
    )
    own_query = own_query[0:1]

    slot_ids = lax.broadcasted_iota(jnp.int32, (pack, slots, 1), 1).reshape(rows, 1)
    is_suffix = slot_ids == suffix_slot
    is_own = slot_ids == 0
    live_mask = lax.broadcasted_iota(jnp.int32, (1, suffix_length), 1) < live
    lane = lax.broadcasted_iota(jnp.int32, (slots, LANES), 1) & (QUERY_HEADS - 1)

    def spread(values):
        width = values.shape[-1]
        return jnp.broadcast_to(values[:, None, :], (pack, slots, width)).reshape(rows, width)

    def contract(left, right):
        return lax.dot_general(
            left, right, (((1,), (1,)), ((), ())), preferred_element_type=jnp.float32
        )

    lse_all = jnp.zeros((slots, LANES), jnp.float32)
    for step in range(steps):
        head = step * pack // group
        columns = slice(head * HEAD_WIDTH, (head + 1) * HEAD_WIDTH)
        heads = [step * pack + i for i in range(pack)]

        def chunk(array, c):
            return array[:, c * HEAD_WIDTH : (c + 1) * HEAD_WIDTH]

        queries = jnp.concatenate([chunk(query_ref, c) for c in heads], axis=0)
        scores = contract(queries, key_ref[:, columns])
        peak = jnp.max(scores, axis=1, keepdims=True)
        weights = jnp.exp2((scores - peak) * EXP2_SCALE)
        total = jnp.sum(weights, axis=1, keepdims=True)
        accum = jnp.dot(
            weights.astype(jnp.bfloat16),
            value_ref[:, columns],
            preferred_element_type=jnp.float32,
        )

        slot_query = jnp.concatenate([chunk(suffix_query, c) for c in heads], axis=0)
        slot_scores = contract(slot_query.astype(jnp.bfloat16), suffix_ref[0, :, columns])
        slot_scores = jnp.where(live_mask, slot_scores, -jnp.inf)
        slot_peak = jnp.max(slot_scores, axis=1, keepdims=True)
        slot_weights = jnp.exp2((slot_scores - slot_peak) * EXP2_SCALE)
        slot_total = jnp.sum(slot_weights, axis=1, keepdims=True)
        slot_accum = jnp.dot(
            slot_weights.astype(jnp.bfloat16),
            suffix_ref[1, :, columns],
            preferred_element_type=jnp.float32,
        )

        new_query = jnp.concatenate([chunk(own_query, c) for c in heads], axis=0)
        new_key = fresh_ref[0, 0:1, columns].astype(jnp.float32)
        new_value = fresh_ref[0, 1:2, columns].astype(jnp.float32)
        new_peak = jnp.sum(new_query * new_key, axis=1, keepdims=True)

        slot_peak = jnp.where(is_suffix, spread(slot_peak), -jnp.inf)
        new_peak = jnp.where(is_own, spread(new_peak), -jnp.inf)
        highest = jnp.maximum(peak, jnp.maximum(slot_peak, new_peak))
        factor = jnp.exp2((peak - highest) * EXP2_SCALE)
        slot_factor = jnp.exp2((slot_peak - highest) * EXP2_SCALE)
        new_factor = jnp.exp2((new_peak - highest) * EXP2_SCALE)
        total = factor * total + slot_factor * spread(slot_total) + new_factor
        accum = factor * accum + slot_factor * spread(slot_accum) + new_factor * new_value
        normed = accum / total
        lse = highest * SCORE_SCALE + jnp.log(total)
        for i, c in enumerate(heads):
            out = normed[i * slots : (i + 1) * slots]
            keep_ref[:, c * HEAD_WIDTH : (c + 1) * HEAD_WIDTH] = out[:half]
            send_ref[:, c * HEAD_WIDTH : (c + 1) * HEAD_WIDTH] = out[half:].astype(jnp.bfloat16)
            lse_all = jnp.where(lane == c, lse[i * slots : (i + 1) * slots], lse_all)
    keep_lse_ref[...] = lse_all[:half]
    first, low = pack_lse(lse_all[half:])
    send_ref[:, OUT_WIDTH : OUT_WIDTH + LANES] = first
    send_ref[:, OUT_WIDTH + LANES : PACK_WIDTH] = low


def merge_kernel(keep_ref, keep_lse_ref, landed_ref, *out_refs, rows):
    lse_keep = keep_lse_ref[...]
    lse_landed = unpack_lse(
        landed_ref[:, OUT_WIDTH : OUT_WIDTH + LANES], landed_ref[:, OUT_WIDTH + LANES : PACK_WIDTH]
    )
    highest = jnp.maximum(lse_keep, lse_landed)
    weight_keep = jnp.exp(lse_keep - highest)
    weight_landed = jnp.exp(lse_landed - highest)
    total = weight_keep + weight_landed
    weight_keep = weight_keep / total
    weight_landed = weight_landed / total
    half = rows // 2
    for c in range(QUERY_HEADS):
        columns = slice(c * HEAD_WIDTH, (c + 1) * HEAD_WIDTH)
        merged = weight_keep[:, c : c + 1] * keep_ref[:, columns] + weight_landed[
            :, c : c + 1
        ] * landed_ref[:, columns].astype(jnp.float32)
        if half:
            out_refs[0][:, columns] = merged[:half]
            out_refs[2][:, columns] = merged[half:].astype(jnp.bfloat16)
        else:
            out_refs[0][:, columns] = merged.astype(jnp.bfloat16)
    if half:
        lse = highest + jnp.log(total)
        out_refs[1][...] = lse[:half]
        first, low = pack_lse(lse[half:])
        out_refs[2][:, OUT_WIDTH : OUT_WIDTH + LANES] = first
        out_refs[2][:, OUT_WIDTH + LANES : PACK_WIDTH] = low


def partial_shapes(rows):
    return (
        jax.ShapeDtypeStruct((rows, OUT_WIDTH), jnp.float32),
        jax.ShapeDtypeStruct((rows, LANES), jnp.float32),
        jax.ShapeDtypeStruct((rows, PACK_WIDTH), jnp.bfloat16),
    )


def per_device(queries, prefix_key_value, suffix_key_value, fresh_key_value, lengths, home):
    slots = lax.axis_size("blk")
    bits = slots.bit_length() - 1
    assert queries.shape[0] == 1 and slots == 1 << bits and slots > 1
    vmem = pl.BlockSpec(memory_space=pltpu.VMEM)
    smem = pl.BlockSpec(memory_space=pltpu.SMEM)
    hbm = pl.BlockSpec(memory_space=pltpu.HBM)

    def swap(array, step):
        return lax.ppermute(array, "blk", [(i, i ^ step) for i in range(slots)])

    half = slots // 2
    landed = swap(queries, half)
    prefix_shape = prefix_key_value.shape
    suffix_shape = suffix_key_value.shape[1:]
    query, fresh, key, value, suffix, live = pl.pallas_call(
        functools.partial(prefetch_kernel, slots=slots),
        out_shape=(
            pltpu.VMEM(queries.shape, jnp.bfloat16),
            pltpu.VMEM(fresh_key_value.shape, jnp.bfloat16),
            pltpu.VMEM(prefix_shape[1:], jnp.bfloat16),
            pltpu.VMEM(prefix_shape[1:], jnp.bfloat16),
            pltpu.VMEM(suffix_shape, jnp.bfloat16),
            pltpu.VMEM((1, LANES), jnp.int32),
        ),
        in_specs=[smem, smem, hbm, hbm, hbm, hbm],
        out_specs=(vmem,) * 6,
        scratch_shapes=[pltpu.SemaphoreType.DMA((2 + 4 * KEY_VALUE_HEADS,))],
        compiler_params=pltpu.CompilerParams(vmem_limit_bytes=PREFETCH_VMEM),
        cost_estimate=pl.CostEstimate(
            flops=0,
            bytes_accessed=2 * (math.prod(prefix_shape) + math.prod(suffix_shape)),
            transcendentals=0,
        ),
        name="prefetch",
    )(
        *(
            pltpu.with_memory_space_constraint(array, pltpu.HBM)
            for array in (
                home,
                lengths,
                queries,
                fresh_key_value,
                prefix_key_value,
                suffix_key_value[0],
            )
        ),
    )
    def join(first, second):
        rows, width = first.shape
        return pl.pallas_call(
            join_kernel,
            out_shape=jax.ShapeDtypeStruct((2 * rows, width), first.dtype),
            in_specs=[vmem, vmem],
            out_specs=vmem,
            compiler_params=pltpu.CompilerParams(vmem_limit_bytes=MERGE_VMEM),
            name="join",
        )(first, second)

    gathered = join(query, landed)
    for i in range(1, bits):
        gathered = join(gathered, swap(gathered, slots >> (i + 1)))

    keep, keep_lse, send = pl.pallas_call(
        functools.partial(attend_kernel, slots=slots),
        out_shape=partial_shapes(half),
        in_specs=[vmem] * 6,
        out_specs=(vmem, vmem, vmem),
        compiler_params=pltpu.CompilerParams(vmem_limit_bytes=ATTEND_VMEM),
        name="attend",
    )(
        *(
            pltpu.with_memory_space_constraint(array, pltpu.VMEM)
            for array in (live, gathered, fresh, key, value, suffix)
        )
    )

    for i in range(bits):
        rows = half >> i
        landed = swap(send, 1 << i)
        if rows > 1:
            shapes = partial_shapes(rows // 2)
        else:
            shapes = (jax.ShapeDtypeStruct((1, OUT_WIDTH), jnp.bfloat16),)
        merged = pl.pallas_call(
            functools.partial(merge_kernel, rows=rows),
            out_shape=shapes,
            in_specs=[vmem, vmem, vmem],
            out_specs=(vmem,) * len(shapes),
            compiler_params=pltpu.CompilerParams(vmem_limit_bytes=MERGE_VMEM),
            name="merge",
        )(keep, keep_lse, landed)
        if rows > 1:
            keep, keep_lse, send = merged
    return merged[0]


def solution(mesh):
    placed = (
        P(("groups", "blk"), None),
        P(None, ("groups", "blk"), None),
        P(("groups", "blk"), None, None, None),
        P(("groups", "blk"), None, None),
        P("groups"),
        P("groups"),
    )
    return jax.shard_map(
        per_device,
        mesh=mesh,
        in_specs=placed,
        out_specs=P(("groups", "blk"), None),
        check_vma=False,
    )
```

```python
import functools
import math

import jax
import jax.numpy as jnp
from jax import lax
from jax.experimental import pallas as pl
from jax.experimental.pallas import tpu as pltpu
from jax.sharding import PartitionSpec as P

QUERY_HEADS = 64
KEY_VALUE_HEADS = 8
HEAD_WIDTH = 128
LANES = 128

OUT_WIDTH = QUERY_HEADS * HEAD_WIDTH
PACK_WIDTH = OUT_WIDTH + 2 * LANES

SCORE_SCALE = HEAD_WIDTH ** (-0.5)
EXP2_SCALE = SCORE_SCALE * math.log2(math.e)

STAGE_BYTES = 16 * 1024 * 1024
MERGE_VMEM = 16 * 1024 * 1024
ATTEND_VMEM = 44 * 1024 * 1024

UNROLLED_STEPS = 8


def pack_lse(lse):
    lane = lax.broadcasted_iota(jnp.int32, lse.shape, 1)
    high = lse.astype(jnp.bfloat16)
    rest = lse - high.astype(jnp.float32)
    middle = rest.astype(jnp.bfloat16)
    low = (rest - middle.astype(jnp.float32)).astype(jnp.bfloat16)
    first = jnp.where(lane < QUERY_HEADS, high.astype(jnp.float32), middle.astype(jnp.float32))
    return first.astype(jnp.bfloat16), low


def unpack_lse(first, low):
    first = first.astype(jnp.float32)
    return first + pltpu.roll(first, QUERY_HEADS, 1) + low.astype(jnp.float32)


def exchange_steps(slots):
    return [(slots >> (i + 1)) | 1 for i in range(slots.bit_length() - 1)]


def slot_of_row(rows, me, slots):
    distance = rows ^ me
    slot, parity = 0, 0
    for i, step in enumerate(exchange_steps(slots)):
        bit = distance if step == 1 else lax.shift_right_logical(distance, step.bit_length() - 1)
        bit = (bit ^ parity if step == 1 else bit) & 1
        parity = parity ^ bit
        slot = slot + bit * (1 << i)
    return slot


def stage_kernel(
    home_hbm, lengths_hbm, query_hbm, fresh_hbm, prefix_hbm, suffix_hbm,
    query_ref, fresh_ref, where_ref, home_buf, lengths_buf, sems, *, slots
):
    pairs = (
        (home_hbm, home_buf),
        (lengths_hbm, lengths_buf),
        (query_hbm, query_ref),
        (fresh_hbm, fresh_ref),
    )
    copies = [
        pltpu.make_async_copy(source, target, sems.at[i])
        for i, (source, target) in enumerate(pairs)
    ]
    for copy in copies:
        copy.start()
    for copy in copies:
        copy.wait()
    me = lax.axis_index("blk")
    here = home_buf[...] == me
    row_ids = lax.broadcasted_iota(jnp.int32, here.shape, 1)

    def pick(values):
        chosen = jnp.where(here, values, 0).astype(jnp.float32)
        return jnp.sum(chosen, axis=1, keepdims=True).astype(jnp.int32)

    lane = lax.broadcasted_iota(jnp.int32, where_ref.shape, 1)
    slot = pick(slot_of_row(row_ids, me, slots))
    where_ref[...] = jnp.where(lane == 0, slot, pick(lengths_buf[...]))


def join_kernel(first_ref, second_ref, out_ref):
    rows = first_ref.shape[0]
    out_ref[:rows] = first_ref[...]
    out_ref[rows:] = second_ref[...]


def attend_kernel(
    where_ref,
    query_ref,
    fresh_ref,
    prefix_ref,
    suffix_ref,
    keep_ref,
    keep_lse_ref,
    send_ref,
    score_buf,
    weight_buf,
    inverse_buf,
    lse_buf,
    part_buf,
    part_lse_buf,
    *,
    slots,
):
    half = slots // 2
    group = QUERY_HEADS // KEY_VALUE_HEADS
    pack = max(1, min(group, LANES // slots))
    per_pair = group // pack
    steps = KEY_VALUE_HEADS // 2 * per_pair
    side = pack * slots
    rows = 2 * side
    prefix_length = prefix_ref.shape[1]
    suffix_length = suffix_ref.shape[2]
    chunks = rows // 16
    chunk_rows = 16
    score_chunks = 4
    chunk_keys = prefix_length // score_chunks

    where_lane = lax.broadcasted_iota(jnp.int32, where_ref.shape, 1)
    places = where_ref[...].astype(jnp.float32)
    suffix_slot = jnp.sum(jnp.where(where_lane == 0, places, 0.0)).astype(jnp.int32)
    live = where_ref[:, 1:2]

    lane = lax.broadcasted_iota(jnp.int32, (slots, LANES), 1) & (QUERY_HEADS - 1)

    def head_columns(head):
        return slice(head * HEAD_WIDTH, (head + 1) * HEAD_WIDTH)

    def contract(left, right):
        return lax.dot_general(
            left, right, (((1,), (1,)), ((), ())), preferred_element_type=jnp.float32
        )

    def columns_at(head):
        return pl.ds(pl.multiple_of(head * HEAD_WIDTH, HEAD_WIDTH), HEAD_WIDTH)

    def pair_columns(pair):
        return pl.ds(pl.multiple_of(pair * 2 * HEAD_WIDTH, 2 * HEAD_WIDTH), 2 * HEAD_WIDTH)

    def query_head(step, member, i):
        head = step // per_pair * 2 + member
        return head * group + step % per_pair * pack + i

    def diagonal(first, second):
        first = jnp.concatenate([first, jnp.zeros_like(first)], axis=1)
        second = jnp.concatenate([jnp.zeros_like(second), second], axis=1)
        return jnp.concatenate([first, second], axis=0)

    def score(step, buffer, chunk):
        queries = diagonal(
            *(
                jnp.concatenate(
                    [query_ref[:, columns_at(query_head(step, member, i))] for i in range(pack)],
                    axis=0,
                )
                for member in range(2)
            )
        )
        keys = slice(chunk * chunk_keys, (chunk + 1) * chunk_keys)
        score_buf[buffer, :, keys] = contract(
            queries, prefix_ref[0, keys, pair_columns(step // per_pair)]
        )

    def weigh(buffer, chunk):
        span = slice(chunk * chunk_rows, (chunk + 1) * chunk_rows)
        scores = score_buf[buffer, span, :]
        peak = jnp.max(scores, axis=1, keepdims=True)
        weights = jnp.exp2(scores * EXP2_SCALE - peak * EXP2_SCALE)
        total = jnp.sum(weights, axis=1, keepdims=True)
        weight_buf[buffer, span, :] = weights.astype(jnp.bfloat16)
        inverse_buf[buffer, span, :] = jnp.broadcast_to(1.0 / total, (chunk_rows, LANES))
        lse_buf[buffer, span, :] = jnp.broadcast_to(
            peak * SCORE_SCALE + jnp.log(total), (chunk_rows, LANES)
        )

    def gather_values(step, buffer, lse_all):
        accum = jnp.dot(
            weight_buf[buffer],
            prefix_ref[1, :, pair_columns(step // per_pair)],
            preferred_element_type=jnp.float32,
        )
        for member in range(2):
            for i in range(pack):
                c = query_head(step, member, i)
                span = slice(member * side + i * slots, member * side + (i + 1) * slots)
                keep_ref[:, columns_at(c)] = (
                    accum[span, member * HEAD_WIDTH : (member + 1) * HEAD_WIDTH]
                    * inverse_buf[buffer, span, :]
                )
                lse_all = jnp.where(lane == c, lse_buf[buffer, span, :], lse_all)
        return lse_all

    sublane = lax.broadcasted_iota(jnp.int32, (group, LANES), 0)
    live_mask = lax.broadcasted_iota(jnp.int32, (1, suffix_length), 1) < live
    picks = lax.broadcasted_iota(jnp.int32, (2 * group, slots), 0)
    slot_ids = lax.broadcasted_iota(jnp.int32, (2 * group, slots), 1)
    chosen = (slot_ids == jnp.where(picks < group, suffix_slot, 0)).astype(jnp.float32)
    chosen = chosen.astype(jnp.bfloat16)
    width = group * HEAD_WIDTH

    def stack(row):
        tile = jnp.zeros((group, HEAD_WIDTH), jnp.float32)
        for i in range(group):
            tile = jnp.where(sublane == i, row[:, head_columns(i)], tile)
        return tile

    def own_parts():
        rows_of = jnp.dot(chosen, query_ref[...], preferred_element_type=jnp.float32)
        stacked = [
            [stack(part[:, h * width : (h + 1) * width]) for h in range(KEY_VALUE_HEADS)]
            for part in (rows_of[:group], rows_of[group:])
        ]
        pairs = range(KEY_VALUE_HEADS // 2)
        queries = [part.astype(jnp.bfloat16) for part in stacked[0]]
        scores = jnp.concatenate(
            [
                contract(
                    diagonal(queries[2 * pair], queries[2 * pair + 1]),
                    suffix_ref[0, 0, :, pair_columns(pair)],
                )
                for pair in pairs
            ],
            axis=0,
        )
        scores = jnp.where(live_mask, scores, -jnp.inf)
        peak = jnp.max(scores, axis=1, keepdims=True)
        weights = jnp.exp2((scores - peak) * EXP2_SCALE)
        total = jnp.sum(weights, axis=1, keepdims=True)
        weights = weights.astype(jnp.bfloat16)
        accum = []
        for pair in pairs:
            both = jnp.dot(
                weights[2 * pair * group : 2 * (pair + 1) * group],
                suffix_ref[0, 1, :, pair_columns(pair)],
                preferred_element_type=jnp.float32,
            )
            accum += [both[:group, :HEAD_WIDTH], both[group:, HEAD_WIDTH:]]
        accum = jnp.concatenate(accum, axis=0)
        part_buf[0] = accum * (1.0 / total)
        part_lse_buf[0] = jnp.broadcast_to(
            peak * SCORE_SCALE + jnp.log(total), (QUERY_HEADS, LANES)
        )

        def per_head(index):
            return jnp.concatenate(
                [
                    jnp.broadcast_to(
                        fresh_ref[0, index : index + 1, head_columns(head)].astype(jnp.float32),
                        (group, HEAD_WIDTH),
                    )
                    for head in range(KEY_VALUE_HEADS)
                ],
                axis=0,
            )

        products = jnp.concatenate(stacked[1], axis=0) * per_head(0)
        lse = jnp.sum(products, axis=1, keepdims=True) * SCORE_SCALE
        part_buf[1] = per_head(1)
        part_lse_buf[1] = jnp.broadcast_to(lse, (QUERY_HEADS, LANES))

    own_parts()
    lse_all = jnp.zeros((slots, LANES), jnp.float32)
    if steps <= UNROLLED_STEPS:
        for step in range(steps + 2):
            for chunk in range(chunks):
                if step < steps and chunk % (chunks // score_chunks) == 0:
                    score(step, step % 2, chunk // (chunks // score_chunks))
                if 1 <= step <= steps:
                    weigh((step - 1) % 2, chunk)
            if step >= 2:
                lse_all = gather_values(step - 2, step % 2, lse_all)
    else:

        def one_step(step, lse_all):
            for chunk in range(score_chunks):
                score(step, 0, chunk)
            for chunk in range(chunks):
                weigh(0, chunk)
            return gather_values(step, 0, lse_all)

        lse_all = lax.fori_loop(0, steps, one_step, lse_all)
    keep_lse_ref[...] = lse_all

    heads = lax.broadcasted_iota(jnp.int32, (QUERY_HEADS, LANES), 0)
    lanes = lax.broadcasted_iota(jnp.int32, (QUERY_HEADS, LANES), 1)
    own = (lanes & (QUERY_HEADS - 1)) == heads

    def merge_row(row, part):
        old = keep_ref[pl.ds(row, 1), :]
        old = jnp.concatenate(
            [stack(old[:, i * width : (i + 1) * width]) for i in range(KEY_VALUE_HEADS)], axis=0
        )
        before = jnp.where(lanes == heads, keep_lse_ref[pl.ds(row, 1), :], 0.0)
        before = jnp.sum(before, axis=1, keepdims=True)
        lse = part_lse_buf[part]
        highest = jnp.maximum(before, lse)
        factor = jnp.exp(before - highest)
        other = jnp.exp(lse - highest)
        total = factor + other
        merged = (factor * old + other * part_buf[part]) * (1.0 / total)
        keep_ref[pl.ds(row, 1), :] = jnp.concatenate(
            [merged[c : c + 1] for c in range(QUERY_HEADS)], axis=1
        )
        new_lse = jnp.where(own, highest + jnp.log(total), 0.0)
        keep_lse_ref[pl.ds(row, 1), :] = jnp.sum(new_lse, axis=0, keepdims=True)

    merge_row(suffix_slot, 0)
    merge_row(0, 1)

    for c in range(QUERY_HEADS):
        send_ref[:, head_columns(c)] = keep_ref[half:, head_columns(c)].astype(jnp.bfloat16)
    first, low = pack_lse(keep_lse_ref[half:])
    send_ref[:, OUT_WIDTH : OUT_WIDTH + LANES] = first
    send_ref[:, OUT_WIDTH + LANES : PACK_WIDTH] = low


def merge_kernel(keep_ref, keep_lse_ref, landed_ref, *out_refs, rows):
    lse_keep = keep_lse_ref[:rows]
    lse_landed = unpack_lse(
        landed_ref[:, OUT_WIDTH : OUT_WIDTH + LANES], landed_ref[:, OUT_WIDTH + LANES : PACK_WIDTH]
    )
    highest = jnp.maximum(lse_keep, lse_landed)
    weight_keep = jnp.exp(lse_keep - highest)
    weight_landed = jnp.exp(lse_landed - highest)
    total = weight_keep + weight_landed
    weight_keep = weight_keep / total
    weight_landed = weight_landed / total
    half = rows // 2
    for c in range(QUERY_HEADS):
        columns = slice(c * HEAD_WIDTH, (c + 1) * HEAD_WIDTH)
        merged = weight_keep[:, c : c + 1] * keep_ref[:rows, columns] + weight_landed[
            :, c : c + 1
        ] * landed_ref[:, columns].astype(jnp.float32)
        if half:
            out_refs[0][:, columns] = merged[:half]
            out_refs[2][:, columns] = merged[half:].astype(jnp.bfloat16)
        else:
            out_refs[0][:, columns] = merged.astype(jnp.bfloat16)
    if half:
        lse = highest + jnp.log(total)
        out_refs[1][...] = lse[:half]
        first, low = pack_lse(lse[half:])
        out_refs[2][:, OUT_WIDTH : OUT_WIDTH + LANES] = first
        out_refs[2][:, OUT_WIDTH + LANES : PACK_WIDTH] = low


def partial_shapes(rows):
    return (
        jax.ShapeDtypeStruct((rows, OUT_WIDTH), jnp.float32),
        jax.ShapeDtypeStruct((rows, LANES), jnp.float32),
        jax.ShapeDtypeStruct((rows, PACK_WIDTH), jnp.bfloat16),
    )


def per_device(queries, prefix_key_value, suffix_key_value, fresh_key_value, lengths, home):
    slots = lax.axis_size("blk")
    bits = slots.bit_length() - 1
    assert queries.shape[0] == 1 and slots == 1 << bits and slots > 1
    vmem = pl.BlockSpec(memory_space=pltpu.VMEM)
    steps = exchange_steps(slots)

    def swap(array, step):
        return lax.ppermute(array, "blk", [(i, i ^ step) for i in range(slots)])

    def in_vmem(*arrays):
        return [pltpu.with_memory_space_constraint(array, pltpu.VMEM) for array in arrays]

    def join(first, second):
        rows, width = first.shape
        return pl.pallas_call(
            join_kernel,
            out_shape=jax.ShapeDtypeStruct((2 * rows, width), first.dtype),
            in_specs=[vmem, vmem],
            out_specs=vmem,
            compiler_params=pltpu.CompilerParams(vmem_limit_bytes=MERGE_VMEM),
            name="join",
        )(*in_vmem(first, second))

    landed = swap(queries, steps[0])
    query, fresh, where = pl.pallas_call(
        functools.partial(stage_kernel, slots=slots),
        out_shape=(
            pltpu.VMEM(queries.shape, jnp.bfloat16),
            pltpu.VMEM(fresh_key_value.shape, jnp.bfloat16),
            pltpu.VMEM((1, LANES), jnp.int32),
        ),
        in_specs=[pl.BlockSpec(memory_space=pltpu.HBM)] * 6,
        out_specs=(vmem,) * 3,
        scratch_shapes=[
            pltpu.VMEM((1, slots), jnp.int32),
            pltpu.VMEM((1, slots), jnp.int32),
            pltpu.SemaphoreType.DMA((4,)),
        ],
        compiler_params=pltpu.CompilerParams(vmem_limit_bytes=MERGE_VMEM),
        cost_estimate=pl.CostEstimate(flops=0, bytes_accessed=STAGE_BYTES, transcendentals=0),
        name="stage",
    )(
        *(
            pltpu.with_memory_space_constraint(array, pltpu.HBM)
            for array in (
                home.reshape(1, slots),
                lengths.reshape(1, slots),
                queries,
                fresh_key_value,
                prefix_key_value,
                suffix_key_value,
            )
        )
    )
    gathered = join(query, landed)
    for step in steps[1:]:
        gathered = join(gathered, swap(gathered, step))

    half = slots // 2
    prefix_length = prefix_key_value.shape[1]
    rows = 2 * max(1, min(QUERY_HEADS // KEY_VALUE_HEADS, LANES // slots)) * slots
    keep, keep_lse, send = pl.pallas_call(
        functools.partial(attend_kernel, slots=slots),
        out_shape=partial_shapes(slots)[:2] + partial_shapes(half)[2:],
        in_specs=[vmem] * 5,
        out_specs=(vmem, vmem, vmem),
        scratch_shapes=[
            pltpu.VMEM((2, rows, prefix_length), jnp.float32),
            pltpu.VMEM((2, rows, prefix_length), jnp.bfloat16),
            pltpu.VMEM((2, rows, LANES), jnp.float32),
            pltpu.VMEM((2, rows, LANES), jnp.float32),
            pltpu.VMEM((2, QUERY_HEADS, LANES), jnp.float32),
            pltpu.VMEM((2, QUERY_HEADS, LANES), jnp.float32),
        ],
        compiler_params=pltpu.CompilerParams(vmem_limit_bytes=ATTEND_VMEM),
        name="attend",
    )(
        *in_vmem(
            where,
            gathered,
            fresh,
            prefix_key_value,
            suffix_key_value,
        )
    )

    for i, step in enumerate(steps[::-1]):
        rows = half >> i
        landed = swap(send, step)
        if rows > 1:
            shapes = partial_shapes(rows // 2)
        else:
            shapes = (jax.ShapeDtypeStruct((1, OUT_WIDTH), jnp.bfloat16),)
        merged = pl.pallas_call(
            functools.partial(merge_kernel, rows=rows),
            out_shape=shapes,
            in_specs=[vmem, vmem, vmem],
            out_specs=(vmem,) * len(shapes),
            compiler_params=pltpu.CompilerParams(vmem_limit_bytes=MERGE_VMEM),
            name="merge",
        )(keep, keep_lse, landed)
        if rows > 1:
            keep, keep_lse, send = merged
    return merged[0]


def solution(mesh):
    placed = (
        P(("groups", "blk"), None),
        P(None, ("groups", "blk"), None),
        P(("groups", "blk"), None, None, None),
        P(("groups", "blk"), None, None),
        P("groups"),
        P("groups"),
    )
    return jax.shard_map(
        per_device,
        mesh=mesh,
        in_specs=placed,
        out_specs=P(("groups", "blk"), None),
        check_vma=False,
    )
```

```python
import functools
import math

import jax
import jax.numpy as jnp
from jax import lax
from jax.experimental import pallas as pl
from jax.experimental.pallas import tpu as pltpu
from jax.sharding import PartitionSpec as P

QUERY_HEADS = 64
KEY_VALUE_HEADS = 8
HEAD_WIDTH = 128
LANES = 128

OUT_WIDTH = QUERY_HEADS * HEAD_WIDTH
PACK_WIDTH = OUT_WIDTH + 2 * LANES

SCORE_SCALE = HEAD_WIDTH ** (-0.5)
EXP2_SCALE = SCORE_SCALE * math.log2(math.e)

STAGE_BYTES = 16 * 1024 * 1024
MERGE_VMEM = 16 * 1024 * 1024
ATTEND_VMEM = 44 * 1024 * 1024

UNROLLED_STEPS = 8
SUFFIX_STEP = 0


def pack_lse(lse):
    lane = lax.broadcasted_iota(jnp.int32, lse.shape, 1)
    high = lse.astype(jnp.bfloat16)
    rest = lse - high.astype(jnp.float32)
    middle = rest.astype(jnp.bfloat16)
    low = (rest - middle.astype(jnp.float32)).astype(jnp.bfloat16)
    first = jnp.where(lane < QUERY_HEADS, high.astype(jnp.float32), middle.astype(jnp.float32))
    return first.astype(jnp.bfloat16), low


def unpack_lse(first, low):
    first = first.astype(jnp.float32)
    return first + pltpu.roll(first, QUERY_HEADS, 1) + low.astype(jnp.float32)


def exchange_steps(slots):
    return [(slots >> (i + 1)) | 1 for i in range(slots.bit_length() - 1)]


def slot_of_row(rows, me, slots):
    distance = rows ^ me
    slot, parity = 0, 0
    for i, step in enumerate(exchange_steps(slots)):
        bit = distance if step == 1 else lax.shift_right_logical(distance, step.bit_length() - 1)
        bit = (bit ^ parity if step == 1 else bit) & 1
        parity = parity ^ bit
        slot = slot + bit * (1 << i)
    return slot


def stage_kernel(
    home_hbm, lengths_hbm, query_hbm, fresh_hbm, prefix_hbm, suffix_hbm,
    query_ref, fresh_ref, where_ref, chosen_ref, home_buf, lengths_buf, sems, *, slots
):
    pairs = (
        (home_hbm, home_buf),
        (lengths_hbm, lengths_buf),
        (query_hbm, query_ref),
        (fresh_hbm, fresh_ref),
    )
    copies = [
        pltpu.make_async_copy(source, target, sems.at[i])
        for i, (source, target) in enumerate(pairs)
    ]
    for copy in copies:
        copy.start()
    for copy in copies:
        copy.wait()
    me = lax.axis_index("blk")
    here = home_buf[...] == me
    row_ids = lax.broadcasted_iota(jnp.int32, here.shape, 1)

    def pick(values):
        chosen = jnp.where(here, values, 0).astype(jnp.float32)
        return jnp.sum(chosen, axis=1, keepdims=True).astype(jnp.int32)

    lane = lax.broadcasted_iota(jnp.int32, where_ref.shape, 1)
    slot = pick(slot_of_row(row_ids, me, slots))
    where_ref[...] = jnp.where(lane == 0, slot, pick(lengths_buf[...]))
    slots_along = lax.broadcasted_iota(jnp.int32, chosen_ref.shape, 1)
    chosen_ref[...] = (slots_along == slot).astype(jnp.float32).astype(jnp.bfloat16)


def join_kernel(*refs):
    rows = refs[0].shape[0]
    for i, ref in enumerate(refs[:-1]):
        refs[-1][i * rows : (i + 1) * rows] = ref[...]


def attend_kernel(
    where_ref,
    chosen_ref,
    query_ref,
    prefix_ref,
    suffix_ref,
    keep_ref,
    keep_lse_ref,
    send_ref,
    score_buf,
    weight_buf,
    inverse_buf,
    lse_buf,
    part_buf,
    part_lse_buf,
    *,
    slots,
):
    half = slots // 2
    group = QUERY_HEADS // KEY_VALUE_HEADS
    pack = max(1, min(group, LANES // slots))
    per_pair = group // pack
    steps = KEY_VALUE_HEADS // 2 * per_pair
    side = pack * slots
    rows = 2 * side
    prefix_length = prefix_ref.shape[1]
    suffix_length = suffix_ref.shape[2]
    chunks = rows // 16
    chunk_rows = 16
    score_chunks = 4
    chunk_keys = prefix_length // score_chunks

    where_lane = lax.broadcasted_iota(jnp.int32, where_ref.shape, 1)
    places = where_ref[...].astype(jnp.float32)
    suffix_slot = jnp.sum(jnp.where(where_lane == 0, places, 0.0)).astype(jnp.int32)
    live = where_ref[:, 1:2]

    lane = lax.broadcasted_iota(jnp.int32, (slots, LANES), 1) & (QUERY_HEADS - 1)

    def head_columns(head):
        return slice(head * HEAD_WIDTH, (head + 1) * HEAD_WIDTH)

    def contract(left, right):
        return lax.dot_general(
            left, right, (((1,), (1,)), ((), ())), preferred_element_type=jnp.float32
        )

    def columns_at(head):
        return pl.ds(pl.multiple_of(head * HEAD_WIDTH, HEAD_WIDTH), HEAD_WIDTH)

    def pair_columns(pair):
        return pl.ds(pl.multiple_of(pair * 2 * HEAD_WIDTH, 2 * HEAD_WIDTH), 2 * HEAD_WIDTH)

    def query_head(step, member, i):
        head = step // per_pair * 2 + member
        return head * group + step % per_pair * pack + i

    def diagonal(first, second):
        first = jnp.concatenate([first, jnp.zeros_like(first)], axis=1)
        second = jnp.concatenate([jnp.zeros_like(second), second], axis=1)
        return jnp.concatenate([first, second], axis=0)

    def score(step, buffer, chunk):
        queries = diagonal(
            *(
                jnp.concatenate(
                    [query_ref[:, columns_at(query_head(step, member, i))] for i in range(pack)],
                    axis=0,
                )
                for member in range(2)
            )
        )
        keys = slice(chunk * chunk_keys, (chunk + 1) * chunk_keys)
        score_buf[buffer, :, keys] = contract(
            queries, prefix_ref[0, keys, pair_columns(step // per_pair)]
        )

    def weigh(buffer, chunk):
        span = slice(chunk * chunk_rows, (chunk + 1) * chunk_rows)
        scores = score_buf[buffer, span, :]
        peak = jnp.max(scores, axis=1, keepdims=True)
        weights = jnp.exp2(scores * EXP2_SCALE - peak * EXP2_SCALE)
        total = jnp.sum(weights, axis=1, keepdims=True)
        weight_buf[buffer, span, :] = weights.astype(jnp.bfloat16)
        inverse_buf[buffer, span, :] = jnp.broadcast_to(1.0 / total, (chunk_rows, LANES))
        lse_buf[buffer, span, :] = jnp.broadcast_to(
            peak * SCORE_SCALE + jnp.log(total), (chunk_rows, LANES)
        )

    def gather_values(step, buffer, lse_all):
        accum = jnp.dot(
            weight_buf[buffer],
            prefix_ref[1, :, pair_columns(step // per_pair)],
            preferred_element_type=jnp.float32,
        )
        for member in range(2):
            for i in range(pack):
                c = query_head(step, member, i)
                span = slice(member * side + i * slots, member * side + (i + 1) * slots)
                keep_ref[:, columns_at(c)] = (
                    accum[span, member * HEAD_WIDTH : (member + 1) * HEAD_WIDTH]
                    * inverse_buf[buffer, span, :]
                )
                lse_all = jnp.where(lane == c, lse_buf[buffer, span, :], lse_all)
        return lse_all

    sublane = lax.broadcasted_iota(jnp.int32, (group, LANES), 0)
    live_mask = lax.broadcasted_iota(jnp.int32, (1, suffix_length), 1) < live
    width = group * HEAD_WIDTH

    def stack(row):
        tile = jnp.zeros((group, HEAD_WIDTH), jnp.float32)
        for i in range(group):
            tile = jnp.where(sublane == i, row[:, head_columns(i)], tile)
        return tile

    def suffix_part():
        rows_of = jnp.dot(chosen_ref[...], query_ref[...], preferred_element_type=jnp.float32)
        queries = [
            stack(rows_of[:group, head * width : (head + 1) * width]).astype(jnp.bfloat16)
            for head in range(KEY_VALUE_HEADS)
        ]
        pairs = range(KEY_VALUE_HEADS // 2)
        scores = jnp.concatenate(
            [
                contract(
                    diagonal(queries[2 * pair], queries[2 * pair + 1]),
                    suffix_ref[0, 0, :, pair_columns(pair)],
                )
                for pair in pairs
            ],
            axis=0,
        )
        scores = jnp.where(live_mask, scores, -jnp.inf)
        peak = jnp.max(scores, axis=1, keepdims=True)
        weights = jnp.exp2((scores - peak) * EXP2_SCALE)
        total = jnp.sum(weights, axis=1, keepdims=True)
        weights = weights.astype(jnp.bfloat16)
        accum = []
        for pair in pairs:
            both = jnp.dot(
                weights[2 * pair * group : 2 * (pair + 1) * group],
                suffix_ref[0, 1, :, pair_columns(pair)],
                preferred_element_type=jnp.float32,
            )
            accum += [both[:group, :HEAD_WIDTH], both[group:, HEAD_WIDTH:]]
        accum = jnp.concatenate(accum, axis=0)
        part_buf[...] = accum * (1.0 / total)
        part_lse_buf[...] = jnp.broadcast_to(
            peak * SCORE_SCALE + jnp.log(total), (QUERY_HEADS, LANES)
        )

    lse_all = jnp.zeros((slots, LANES), jnp.float32)
    if steps <= UNROLLED_STEPS:
        for step in range(steps + 2):
            if step == SUFFIX_STEP:
                suffix_part()
            for chunk in range(chunks):
                if step < steps and chunk % (chunks // score_chunks) == 0:
                    score(step, step % 2, chunk // (chunks // score_chunks))
                if 1 <= step <= steps:
                    weigh((step - 1) % 2, chunk)
            if step >= 2:
                lse_all = gather_values(step - 2, step % 2, lse_all)
    else:
        suffix_part()

        def one_step(step, lse_all):
            for chunk in range(score_chunks):
                score(step, 0, chunk)
            for chunk in range(chunks):
                weigh(0, chunk)
            return gather_values(step, 0, lse_all)

        lse_all = lax.fori_loop(0, steps, one_step, lse_all)
    keep_lse_ref[...] = lse_all

    heads = lax.broadcasted_iota(jnp.int32, (QUERY_HEADS, LANES), 0)
    lanes = lax.broadcasted_iota(jnp.int32, (QUERY_HEADS, LANES), 1)
    own = (lanes & (QUERY_HEADS - 1)) == heads

    old = keep_ref[pl.ds(suffix_slot, 1), :]
    old = jnp.concatenate(
        [stack(old[:, i * width : (i + 1) * width]) for i in range(KEY_VALUE_HEADS)], axis=0
    )
    before = jnp.where(lanes == heads, keep_lse_ref[pl.ds(suffix_slot, 1), :], 0.0)
    before = jnp.sum(before, axis=1, keepdims=True)
    lse = part_lse_buf[...]
    highest = jnp.maximum(before, lse)
    factor = jnp.exp(before - highest)
    other = jnp.exp(lse - highest)
    total = factor + other
    merged = (factor * old + other * part_buf[...]) * (1.0 / total)
    keep_ref[pl.ds(suffix_slot, 1), :] = jnp.concatenate(
        [merged[c : c + 1] for c in range(QUERY_HEADS)], axis=1
    )
    new_lse = jnp.where(own, highest + jnp.log(total), 0.0)
    keep_lse_ref[pl.ds(suffix_slot, 1), :] = jnp.sum(new_lse, axis=0, keepdims=True)

    for c in range(QUERY_HEADS):
        send_ref[:, head_columns(c)] = keep_ref[half:, head_columns(c)].astype(jnp.bfloat16)
    first, low = pack_lse(keep_lse_ref[half:])
    send_ref[:, OUT_WIDTH : OUT_WIDTH + LANES] = first
    send_ref[:, OUT_WIDTH + LANES : PACK_WIDTH] = low


def fresh_kernel(query_ref, fresh_ref, keep_ref, keep_lse_ref, out_ref, out_lse_ref):
    lane = lax.broadcasted_iota(jnp.int32, (1, LANES), 1) & (QUERY_HEADS - 1)
    group = QUERY_HEADS // KEY_VALUE_HEADS
    lse_new = jnp.zeros((1, LANES), jnp.float32)
    for c in range(QUERY_HEADS):
        columns = slice(c * HEAD_WIDTH, (c + 1) * HEAD_WIDTH)
        head = c // group
        key = fresh_ref[0, 0:1, head * HEAD_WIDTH : (head + 1) * HEAD_WIDTH].astype(jnp.float32)
        query = query_ref[:, columns].astype(jnp.float32)
        lse_new = jnp.where(lane == c, jnp.sum(query * key, axis=1, keepdims=True), lse_new)
    lse_new = lse_new * SCORE_SCALE
    lse_keep = keep_lse_ref[...]
    highest = jnp.maximum(lse_keep, lse_new)
    weight_keep = jnp.exp(lse_keep - highest)
    weight_new = jnp.exp(lse_new - highest)
    total = weight_keep + weight_new
    weight_keep = weight_keep / total
    weight_new = weight_new / total
    for c in range(QUERY_HEADS):
        columns = slice(c * HEAD_WIDTH, (c + 1) * HEAD_WIDTH)
        head = c // group
        value = fresh_ref[0, 1:2, head * HEAD_WIDTH : (head + 1) * HEAD_WIDTH].astype(jnp.float32)
        out_ref[:, columns] = (
            weight_keep[:, c : c + 1] * keep_ref[:, columns] + weight_new[:, c : c + 1] * value
        )
    out_lse_ref[...] = highest + jnp.log(total)


def merge_kernel(keep_ref, keep_lse_ref, *refs, rows, parts, landings):
    landed_refs, out_refs = refs[:landings], refs[landings:]
    lses = [keep_lse_ref[:rows]] + [
        unpack_lse(ref[:, OUT_WIDTH : OUT_WIDTH + LANES], ref[:, OUT_WIDTH + LANES : PACK_WIDTH])
        for ref in landed_refs
    ]
    highest = functools.reduce(jnp.maximum, lses)
    weights = [jnp.exp(lse - highest) for lse in lses]
    total = functools.reduce(jnp.add, weights)
    weights = [weight / total for weight in weights]
    size = rows // parts
    for c in range(QUERY_HEADS):
        columns = slice(c * HEAD_WIDTH, (c + 1) * HEAD_WIDTH)
        merged = weights[0][:, c : c + 1] * keep_ref[:rows, columns]
        for weight, ref in zip(weights[1:], landed_refs):
            merged = merged + weight[:, c : c + 1] * ref[:, columns].astype(jnp.float32)
        if parts == 1:
            out_refs[0][:, columns] = merged.astype(jnp.bfloat16)
        else:
            out_refs[0][:, columns] = merged[:size]
            for i in range(1, parts):
                piece = merged[i * size : (i + 1) * size]
                out_refs[1 + i][:, columns] = piece.astype(jnp.bfloat16)
    if parts > 1:
        lse = highest + jnp.log(total)
        out_refs[1][...] = lse[:size]
        for i in range(1, parts):
            first, low = pack_lse(lse[i * size : (i + 1) * size])
            out_refs[1 + i][:, OUT_WIDTH : OUT_WIDTH + LANES] = first
            out_refs[1 + i][:, OUT_WIDTH + LANES : PACK_WIDTH] = low


def partial_shapes(rows):
    return (
        jax.ShapeDtypeStruct((rows, OUT_WIDTH), jnp.float32),
        jax.ShapeDtypeStruct((rows, LANES), jnp.float32),
        jax.ShapeDtypeStruct((rows, PACK_WIDTH), jnp.bfloat16),
    )


def per_device(queries, prefix_key_value, suffix_key_value, fresh_key_value, lengths, home):
    slots = lax.axis_size("blk")
    bits = slots.bit_length() - 1
    assert queries.shape[0] == 1 and slots == 1 << bits and slots > 1
    vmem = pl.BlockSpec(memory_space=pltpu.VMEM)
    steps = exchange_steps(slots)

    def swap(array, step):
        return lax.ppermute(array, "blk", [(i, i ^ step) for i in range(slots)])

    def in_vmem(*arrays):
        return [pltpu.with_memory_space_constraint(array, pltpu.VMEM) for array in arrays]

    def join(*arrays):
        rows, width = arrays[0].shape
        return pl.pallas_call(
            join_kernel,
            out_shape=jax.ShapeDtypeStruct((len(arrays) * rows, width), arrays[0].dtype),
            in_specs=[vmem] * len(arrays),
            out_specs=vmem,
            compiler_params=pltpu.CompilerParams(vmem_limit_bytes=MERGE_VMEM),
            name="join",
        )(*in_vmem(*arrays))

    phases = [[step] for step in steps]
    if bits > 3:
        phases = phases[:-3] + [steps[-3:-1]] + phases[-1:]

    def partners(phase):
        return phase if len(phase) == 1 else [phase[0], phase[1], phase[0] ^ phase[1]]

    def exchange(arrays, distances):
        order = sorted(range(len(distances)), key=lambda i: distances[i])
        landed = {i: swap(arrays[i], distances[i]) for i in order}
        return [landed[i] for i in range(len(distances))]

    landed = swap(queries, steps[0])
    query, fresh, where, chosen = pl.pallas_call(
        functools.partial(stage_kernel, slots=slots),
        out_shape=(
            pltpu.VMEM(queries.shape, jnp.bfloat16),
            pltpu.VMEM(fresh_key_value.shape, jnp.bfloat16),
            pltpu.VMEM((1, LANES), jnp.int32),
            pltpu.VMEM((16, slots), jnp.bfloat16),
        ),
        in_specs=[pl.BlockSpec(memory_space=pltpu.HBM)] * 6,
        out_specs=(vmem,) * 4,
        scratch_shapes=[
            pltpu.VMEM((1, slots), jnp.int32),
            pltpu.VMEM((1, slots), jnp.int32),
            pltpu.SemaphoreType.DMA((4,)),
        ],
        compiler_params=pltpu.CompilerParams(vmem_limit_bytes=MERGE_VMEM),
        cost_estimate=pl.CostEstimate(flops=0, bytes_accessed=STAGE_BYTES, transcendentals=0),
        name="stage",
    )(
        *(
            pltpu.with_memory_space_constraint(array, pltpu.HBM)
            for array in (
                home.reshape(1, slots),
                lengths.reshape(1, slots),
                queries,
                fresh_key_value,
                prefix_key_value,
                suffix_key_value,
            )
        )
    )
    gathered = join(query, landed)
    for phase in phases[1:]:
        landed = exchange([gathered] * len(partners(phase)), partners(phase))
        gathered = join(gathered, *landed)

    half = slots // 2
    prefix_length = prefix_key_value.shape[1]
    rows = 2 * max(1, min(QUERY_HEADS // KEY_VALUE_HEADS, LANES // slots)) * slots
    keep, keep_lse, send = pl.pallas_call(
        functools.partial(attend_kernel, slots=slots),
        out_shape=partial_shapes(slots)[:2] + partial_shapes(half)[2:],
        in_specs=[vmem] * 5,
        out_specs=(vmem, vmem, vmem),
        scratch_shapes=[
            pltpu.VMEM((2, rows, prefix_length), jnp.float32),
            pltpu.VMEM((2, rows, prefix_length), jnp.bfloat16),
            pltpu.VMEM((2, rows, LANES), jnp.float32),
            pltpu.VMEM((2, rows, LANES), jnp.float32),
            pltpu.VMEM((QUERY_HEADS, LANES), jnp.float32),
            pltpu.VMEM((QUERY_HEADS, LANES), jnp.float32),
        ],
        compiler_params=pltpu.CompilerParams(vmem_limit_bytes=ATTEND_VMEM),
        name="attend",
    )(
        *in_vmem(
            where,
            chosen,
            gathered,
            prefix_key_value,
            suffix_key_value,
        )
    )

    sends = [send]
    rows = half
    for i, phase in enumerate(phases[::-1]):
        landed = exchange(sends, partners(phase))
        if i == len(phases) - 1:
            parts, shapes = 1, (jax.ShapeDtypeStruct((1, OUT_WIDTH), jnp.bfloat16),)
            keep, keep_lse = pl.pallas_call(
                fresh_kernel,
                out_shape=partial_shapes(1)[:2],
                in_specs=[vmem] * 4,
                out_specs=(vmem,) * 2,
                compiler_params=pltpu.CompilerParams(vmem_limit_bytes=MERGE_VMEM),
                cost_estimate=pl.CostEstimate(
                    flops=0, bytes_accessed=STAGE_BYTES // 8, transcendentals=0
                ),
                name="fresh",
            )(*in_vmem(query, fresh, keep, keep_lse))
        else:
            parts = 1 << len(phases[-2 - i])
            shapes = partial_shapes(rows // parts)
            shapes = shapes[:2] + shapes[2:] * (parts - 1)
        merged = pl.pallas_call(
            functools.partial(merge_kernel, rows=rows, parts=parts, landings=len(landed)),
            out_shape=shapes,
            in_specs=[vmem] * (2 + len(landed)),
            out_specs=(vmem,) * len(shapes),
            compiler_params=pltpu.CompilerParams(vmem_limit_bytes=MERGE_VMEM),
            name="merge",
        )(keep, keep_lse, *landed[::-1])
        if parts > 1:
            keep, keep_lse, *sends = merged
            rows = rows // parts
    return merged[0]


def solution(mesh):
    placed = (
        P(("groups", "blk"), None),
        P(None, ("groups", "blk"), None),
        P(("groups", "blk"), None, None, None),
        P(("groups", "blk"), None, None),
        P("groups"),
        P("groups"),
    )
    return jax.shard_map(
        per_device,
        mesh=mesh,
        in_specs=placed,
        out_specs=P(("groups", "blk"), None),
        check_vma=False,
    )
```

```python
import functools
import math

import jax
import jax.numpy as jnp
from jax import lax
from jax.experimental import pallas as pl
from jax.experimental.pallas import tpu as pltpu
from jax.sharding import PartitionSpec as P

QUERY_HEADS = 64
KEY_VALUE_HEADS = 8
HEAD_WIDTH = 128
LANES = 128
GROUP = QUERY_HEADS // KEY_VALUE_HEADS
OUT_WIDTH = QUERY_HEADS * HEAD_WIDTH

BLOCK_ROWS = QUERY_HEADS + 8

SCORE_SCALE = HEAD_WIDTH ** (-0.5)
EXP2_SCALE = SCORE_SCALE * math.log2(math.e)

STAGE_BYTES = 16 * 1024 * 1024
MERGE_VMEM = 16 * 1024 * 1024
ATTEND_VMEM = 44 * 1024 * 1024
UNROLLED_STEPS = 8


def columns_at(head):
    if isinstance(head, int):
        return slice(head * HEAD_WIDTH, (head + 1) * HEAD_WIDTH)
    return pl.ds(pl.multiple_of(head * HEAD_WIDTH, HEAD_WIDTH), HEAD_WIDTH)


def iota(shape, dimension):
    return lax.broadcasted_iota(jnp.int32, shape, dimension)


def heads_down(row):
    sublane = iota((GROUP, HEAD_WIDTH), 0)
    tiles = []
    for head in range(KEY_VALUE_HEADS):
        tile = jnp.zeros((GROUP, HEAD_WIDTH), jnp.float32)
        for i in range(GROUP):
            tile = jnp.where(sublane == i, row[:, columns_at(head * GROUP + i)], tile)
        tiles.append(tile)
    return jnp.concatenate(tiles, axis=0)


def spread_heads(row):
    return jnp.concatenate(
        [
            jnp.broadcast_to(row[:, columns_at(head)], (GROUP, HEAD_WIDTH))
            for head in range(KEY_VALUE_HEADS)
        ],
        axis=0,
    )


def pack_lse(lse):
    shape = (QUERY_HEADS, LANES)
    own = (iota(shape, 1) & (QUERY_HEADS - 1)) == iota(shape, 0)
    along = jnp.sum(jnp.where(own, lse, 0.0), axis=0, keepdims=True)
    high = along.astype(jnp.bfloat16).astype(jnp.float32)
    rest = along - high
    middle = rest.astype(jnp.bfloat16).astype(jnp.float32)
    low = rest - middle
    tile = (8, LANES)
    first = jnp.where(iota(tile, 1) < QUERY_HEADS, high, middle)
    return jnp.where(iota(tile, 0) < 4, first, low).astype(jnp.bfloat16)


def unpack_lse(tile):
    tile = tile.astype(jnp.float32)
    first = tile[0:1]
    along = first + pltpu.roll(first, QUERY_HEADS, 1) + tile[4:5]
    shape = (QUERY_HEADS, LANES)
    chosen = jnp.where(iota(shape, 1) == iota(shape, 0), along, 0.0)
    return jnp.sum(chosen, axis=1, keepdims=True)


def exchange_steps(slots):
    return [(slots >> (i + 1)) | 1 for i in range(slots.bit_length() - 1)]


def slot_of_row(rows, me, slots):
    distance = rows ^ me
    slot, parity = 0, 0
    for i, step in enumerate(exchange_steps(slots)):
        bit = distance if step == 1 else lax.shift_right_logical(distance, step.bit_length() - 1)
        bit = (bit ^ parity if step == 1 else bit) & 1
        parity = parity ^ bit
        slot = slot + bit * (1 << i)
    return slot


def for_rows(count, body):
    if count <= 16:
        for row in range(count):
            body(row)
    else:

        def one(row, carry):
            body(row)
            return carry

        lax.fori_loop(0, count, one, 0)


def stage_kernel(
    home_hbm, lengths_hbm, query_hbm, fresh_hbm, prefix_hbm, suffix_hbm,
    query_ref, fresh_ref, where_ref, home_buf, lengths_buf, query_buf, sems, *, slots
):
    pairs = (
        (home_hbm, home_buf),
        (lengths_hbm, lengths_buf),
        (query_hbm, query_buf),
        (fresh_hbm, fresh_ref),
    )
    copies = [
        pltpu.make_async_copy(source, target, sems.at[i])
        for i, (source, target) in enumerate(pairs)
    ]
    for copy in copies:
        copy.start()
    for copy in copies:
        copy.wait()
    me = lax.axis_index("blk")
    here = home_buf[...] == me
    row_ids = iota(here.shape, 1)

    def pick(values):
        chosen = jnp.where(here, values, 0).astype(jnp.float32)
        return jnp.sum(chosen, axis=1, keepdims=True).astype(jnp.int32)

    slot = pick(slot_of_row(row_ids, me, slots))
    where_ref[...] = jnp.where(iota(where_ref.shape, 1) == 0, slot, pick(lengths_buf[...]))
    query_ref[0] = heads_down(query_buf[...].astype(jnp.float32)).astype(jnp.bfloat16)


def first_join_kernel(query_ref, landed_ref, out_ref):
    out_ref[0] = query_ref[0]
    out_ref[1] = heads_down(landed_ref[...].astype(jnp.float32)).astype(jnp.bfloat16)


def join_kernel(*refs):
    rows = refs[0].shape[0]
    for i, ref in enumerate(refs[:-1]):
        refs[-1][i * rows : (i + 1) * rows] = ref[...]


def attend_kernel(
    where_ref,
    query_ref,
    prefix_ref,
    suffix_ref,
    keep_ref,
    keep_lse_ref,
    send_ref,
    score_buf,
    weight_buf,
    inverse_buf,
    part_buf,
    part_lse_buf,
    *,
    slots,
):
    half = slots // 2
    block = min(slots, LANES // GROUP)
    blocks = slots // block
    steps = KEY_VALUE_HEADS // 2 * blocks
    side = block * GROUP
    rows = 2 * side
    prefix_length = prefix_ref.shape[1]
    suffix_length = suffix_ref.shape[2]
    chunk_rows = 2 * GROUP
    chunks = rows // chunk_rows
    score_chunks = 4
    chunk_keys = prefix_length // score_chunks

    places = where_ref[...].astype(jnp.float32)
    suffix_slot = jnp.sum(jnp.where(iota(places.shape, 1) == 0, places, 0.0)).astype(jnp.int32)
    live = where_ref[:, 1:2]

    def contract(left, right):
        return lax.dot_general(
            left, right, (((1,), (1,)), ((), ())), preferred_element_type=jnp.float32
        )

    def pair_columns(pair):
        if isinstance(pair, int):
            return slice(pair * 2 * HEAD_WIDTH, (pair + 1) * 2 * HEAD_WIDTH)
        return pl.ds(pl.multiple_of(pair * 2 * HEAD_WIDTH, 2 * HEAD_WIDTH), 2 * HEAD_WIDTH)

    def group_rows(head):
        if isinstance(head, int):
            return slice(head * GROUP, (head + 1) * GROUP)
        return pl.ds(pl.multiple_of(head * GROUP, GROUP), GROUP)

    def block_rows(step):
        start = step % blocks * block
        return slice(start, start + block) if isinstance(start, int) else pl.ds(start, block)

    def diagonal(first, second):
        first = jnp.concatenate([first, jnp.zeros_like(first)], axis=1)
        second = jnp.concatenate([jnp.zeros_like(second), second], axis=1)
        return jnp.concatenate([first, second], axis=0).astype(jnp.bfloat16)

    def score(step, buffer, chunk):
        pair = step // blocks
        queries = diagonal(
            *(
                query_ref[block_rows(step), group_rows(2 * pair + member), :]
                .astype(jnp.float32)
                .reshape(side, HEAD_WIDTH)
                for member in range(2)
            )
        )
        keys = slice(chunk * chunk_keys, (chunk + 1) * chunk_keys)
        score_buf[buffer, :, keys] = contract(queries, prefix_ref[0, keys, pair_columns(pair)])

    def weigh(step, buffer, chunk):
        span = slice(chunk * chunk_rows, (chunk + 1) * chunk_rows)
        scores = score_buf[buffer, span, :]
        peak = jnp.max(scores, axis=1, keepdims=True)
        weights = jnp.exp2(scores * EXP2_SCALE - peak * EXP2_SCALE)
        total = jnp.sum(weights, axis=1, keepdims=True)
        weight_buf[buffer, span, :] = weights.astype(jnp.bfloat16)
        inverse_buf[buffer, span, :] = jnp.broadcast_to(1.0 / total, (chunk_rows, LANES))
        lse = jnp.broadcast_to(peak * SCORE_SCALE + jnp.log(total), (chunk_rows, LANES))
        head = step // blocks * 2 + chunk * chunk_rows // side
        slot = step % blocks * block + chunk * chunk_rows % side // GROUP
        keep_lse_ref[slot, group_rows(head), :] = lse[:GROUP]
        keep_lse_ref[slot + 1, group_rows(head), :] = lse[GROUP:]

    def gather_values(step, buffer):
        pair = step // blocks
        accum = jnp.dot(
            weight_buf[buffer],
            prefix_ref[1, :, pair_columns(pair)],
            preferred_element_type=jnp.float32,
        )
        for member in range(2):
            span = slice(member * side, (member + 1) * side)
            normed = accum[span, columns_at(member)] * inverse_buf[buffer, span, :]
            keep_ref[block_rows(step), group_rows(2 * pair + member), :] = normed.reshape(
                block, GROUP, HEAD_WIDTH
            )

    def suffix_part():
        query = query_ref[suffix_slot].astype(jnp.float32)
        pairs = range(KEY_VALUE_HEADS // 2)
        scores = jnp.concatenate(
            [
                contract(
                    diagonal(query[group_rows(2 * pair)], query[group_rows(2 * pair + 1)]),
                    suffix_ref[0, 0, :, pair_columns(pair)],
                )
                for pair in pairs
            ],
            axis=0,
        )
        scores = jnp.where(iota((1, suffix_length), 1) < live, scores, -jnp.inf)
        peak = jnp.max(scores, axis=1, keepdims=True)
        weights = jnp.exp2((scores - peak) * EXP2_SCALE)
        total = jnp.sum(weights, axis=1, keepdims=True)
        weights = weights.astype(jnp.bfloat16)
        accum = []
        for pair in pairs:
            both = jnp.dot(
                weights[2 * pair * GROUP : 2 * (pair + 1) * GROUP],
                suffix_ref[0, 1, :, pair_columns(pair)],
                preferred_element_type=jnp.float32,
            )
            accum += [both[:GROUP, :HEAD_WIDTH], both[GROUP:, HEAD_WIDTH:]]
        part_buf[...] = jnp.concatenate(accum, axis=0) * (1.0 / total)
        part_lse_buf[...] = jnp.broadcast_to(
            peak * SCORE_SCALE + jnp.log(total), (QUERY_HEADS, LANES)
        )

    suffix_part()
    if steps <= UNROLLED_STEPS:
        for step in range(steps + 2):
            for chunk in range(chunks):
                if step < steps and chunk % (chunks // score_chunks) == 0:
                    score(step, step % 2, chunk // (chunks // score_chunks))
                if 1 <= step <= steps:
                    weigh(step - 1, (step - 1) % 2, chunk)
            if step >= 2:
                gather_values(step - 2, step % 2)
    else:

        def one_step(step, carry):
            for chunk in range(score_chunks):
                score(step, 0, chunk)
            for chunk in range(chunks):
                weigh(step, 0, chunk)
            gather_values(step, 0)
            return carry

        lax.fori_loop(0, steps, one_step, 0)

    before = keep_lse_ref[suffix_slot]
    lse = part_lse_buf[...]
    highest = jnp.maximum(before, lse)
    factor = jnp.exp(before - highest)
    other = jnp.exp(lse - highest)
    total = factor + other
    merged = (factor * keep_ref[suffix_slot] + other * part_buf[...]) * (1.0 / total)
    keep_ref[suffix_slot] = merged
    keep_lse_ref[suffix_slot] = highest + jnp.log(total)

    def write(row):
        send_ref[row, :QUERY_HEADS] = keep_ref[half + row].astype(jnp.bfloat16)
        send_ref[row, QUERY_HEADS:] = pack_lse(keep_lse_ref[half + row])

    for_rows(half, write)


def merge_parts(lses, values):
    highest = functools.reduce(jnp.maximum, lses)
    weights = [jnp.exp(lse - highest) for lse in lses]
    total = functools.reduce(jnp.add, weights)
    merged = functools.reduce(jnp.add, [w * value for w, value in zip(weights, values)])
    return merged * (1.0 / total), highest + jnp.log(total)


def fresh_kernel(query_ref, fresh_ref, keep_ref, keep_lse_ref, out_ref, out_lse_ref):
    key = spread_heads(fresh_ref[0, 0:1, :].astype(jnp.float32))
    value = spread_heads(fresh_ref[0, 1:2, :].astype(jnp.float32))
    products = query_ref[0].astype(jnp.float32) * key
    lse = jnp.sum(products, axis=1, keepdims=True) * SCORE_SCALE
    out_ref[0], out_lse_ref[0] = merge_parts([keep_lse_ref[0], lse], [keep_ref[0], value])


def merge_kernel(keep_ref, keep_lse_ref, *refs, rows, parts, landings):
    landed_refs, out_refs = refs[:landings], refs[landings:]
    size = rows // parts

    def merge(row):
        lses = [keep_lse_ref[row]] + [unpack_lse(ref[row, QUERY_HEADS:]) for ref in landed_refs]
        values = [keep_ref[row]] + [
            ref[row, :QUERY_HEADS].astype(jnp.float32) for ref in landed_refs
        ]
        return merge_parts(lses, values)

    if parts == 1:
        merged, _ = merge(0)
        for c in range(QUERY_HEADS):
            out_refs[0][:, columns_at(c)] = merged[c : c + 1].astype(jnp.bfloat16)
        return

    def keep(row):
        out_refs[0][row], out_refs[1][row] = merge(row)

    for_rows(size, keep)
    for i in range(1, parts):

        def send(row):
            merged, lse = merge(i * size + row)
            out_refs[1 + i][row, :QUERY_HEADS] = merged.astype(jnp.bfloat16)
            out_refs[1 + i][row, QUERY_HEADS:] = pack_lse(lse)

        for_rows(size, send)


def partial_shapes(rows):
    return (
        jax.ShapeDtypeStruct((rows, QUERY_HEADS, HEAD_WIDTH), jnp.float32),
        jax.ShapeDtypeStruct((rows, QUERY_HEADS, LANES), jnp.float32),
        jax.ShapeDtypeStruct((rows, BLOCK_ROWS, HEAD_WIDTH), jnp.bfloat16),
    )


def per_device(queries, prefix_key_value, suffix_key_value, fresh_key_value, lengths, home):
    slots = lax.axis_size("blk")
    bits = slots.bit_length() - 1
    assert queries.shape[0] == 1 and slots == 1 << bits and slots > 1
    vmem = pl.BlockSpec(memory_space=pltpu.VMEM)
    steps = exchange_steps(slots)

    def swap(array, step):
        return lax.ppermute(array, "blk", [(i, i ^ step) for i in range(slots)])

    def in_vmem(*arrays):
        return [pltpu.with_memory_space_constraint(array, pltpu.VMEM) for array in arrays]

    def join(kernel, rows, *arrays):
        return pl.pallas_call(
            kernel,
            out_shape=jax.ShapeDtypeStruct((rows, QUERY_HEADS, HEAD_WIDTH), jnp.bfloat16),
            in_specs=[vmem] * len(arrays),
            out_specs=vmem,
            compiler_params=pltpu.CompilerParams(vmem_limit_bytes=MERGE_VMEM),
            name="join",
        )(*in_vmem(*arrays))

    phases = [[step] for step in steps]
    if bits > 3:
        phases = phases[:-3] + [steps[-3:-1]] + phases[-1:]

    def partners(phase):
        return phase if len(phase) == 1 else [phase[0], phase[1], phase[0] ^ phase[1]]

    def exchange(arrays, distances):
        order = sorted(range(len(distances)), key=lambda i: distances[i])
        landed = {i: swap(arrays[i], distances[i]) for i in order}
        return [landed[i] for i in range(len(distances))]

    landed = swap(queries, steps[0])
    query, fresh, where = pl.pallas_call(
        functools.partial(stage_kernel, slots=slots),
        out_shape=(
            pltpu.VMEM((1, QUERY_HEADS, HEAD_WIDTH), jnp.bfloat16),
            pltpu.VMEM(fresh_key_value.shape, jnp.bfloat16),
            pltpu.VMEM((1, LANES), jnp.int32),
        ),
        in_specs=[pl.BlockSpec(memory_space=pltpu.HBM)] * 6,
        out_specs=(vmem,) * 3,
        scratch_shapes=[
            pltpu.VMEM((1, slots), jnp.int32),
            pltpu.VMEM((1, slots), jnp.int32),
            pltpu.VMEM(queries.shape, jnp.bfloat16),
            pltpu.SemaphoreType.DMA((4,)),
        ],
        compiler_params=pltpu.CompilerParams(vmem_limit_bytes=MERGE_VMEM),
        cost_estimate=pl.CostEstimate(flops=0, bytes_accessed=STAGE_BYTES, transcendentals=0),
        name="stage",
    )(
        *(
            pltpu.with_memory_space_constraint(array, pltpu.HBM)
            for array in (
                home.reshape(1, slots),
                lengths.reshape(1, slots),
                queries,
                fresh_key_value,
                prefix_key_value,
                suffix_key_value,
            )
        )
    )
    gathered = join(first_join_kernel, 2, query, landed)
    for phase in phases[1:]:
        landed = exchange([gathered] * len(partners(phase)), partners(phase))
        gathered = join(join_kernel, gathered.shape[0] << len(phase), gathered, *landed)

    half = slots // 2
    prefix_length = prefix_key_value.shape[1]
    rows = 2 * GROUP * min(slots, LANES // GROUP)
    keep, keep_lse, send = pl.pallas_call(
        functools.partial(attend_kernel, slots=slots),
        out_shape=partial_shapes(slots)[:2] + partial_shapes(half)[2:],
        in_specs=[vmem] * 4,
        out_specs=(vmem, vmem, vmem),
        scratch_shapes=[
            pltpu.VMEM((2, rows, prefix_length), jnp.float32),
            pltpu.VMEM((2, rows, prefix_length), jnp.bfloat16),
            pltpu.VMEM((2, rows, LANES), jnp.float32),
            pltpu.VMEM((QUERY_HEADS, LANES), jnp.float32),
            pltpu.VMEM((QUERY_HEADS, LANES), jnp.float32),
        ],
        compiler_params=pltpu.CompilerParams(vmem_limit_bytes=ATTEND_VMEM),
        name="attend",
    )(*in_vmem(where, gathered, prefix_key_value, suffix_key_value))

    sends = [send]
    rows = half
    for i, phase in enumerate(phases[::-1]):
        landed = exchange(sends, partners(phase))
        if i == len(phases) - 1:
            parts, shapes = 1, (jax.ShapeDtypeStruct((1, OUT_WIDTH), jnp.bfloat16),)
            keep, keep_lse = pl.pallas_call(
                fresh_kernel,
                out_shape=partial_shapes(1)[:2],
                in_specs=[vmem] * 4,
                out_specs=(vmem,) * 2,
                compiler_params=pltpu.CompilerParams(vmem_limit_bytes=MERGE_VMEM),
                cost_estimate=pl.CostEstimate(
                    flops=0, bytes_accessed=STAGE_BYTES // 8, transcendentals=0
                ),
                name="fresh",
            )(*in_vmem(query, fresh, keep, keep_lse))
        else:
            parts = 1 << len(phases[-2 - i])
            shapes = partial_shapes(rows // parts)
            shapes = shapes[:2] + shapes[2:] * (parts - 1)
        merged = pl.pallas_call(
            functools.partial(merge_kernel, rows=rows, parts=parts, landings=len(landed)),
            out_shape=shapes,
            in_specs=[vmem] * (2 + len(landed)),
            out_specs=(vmem,) * len(shapes),
            compiler_params=pltpu.CompilerParams(vmem_limit_bytes=MERGE_VMEM),
            name="merge",
        )(keep, keep_lse, *landed[::-1])
        if parts > 1:
            keep, keep_lse, *sends = merged
            rows = rows // parts
    return merged[0]


def solution(mesh):
    placed = (
        P(("groups", "blk"), None),
        P(None, ("groups", "blk"), None),
        P(("groups", "blk"), None, None, None),
        P(("groups", "blk"), None, None),
        P("groups"),
        P("groups"),
    )
    return jax.shard_map(
        per_device,
        mesh=mesh,
        in_specs=placed,
        out_specs=P(("groups", "blk"), None),
        check_vma=False,
    )
```

```python
import functools
import math

import jax
import jax.numpy as jnp
from jax import lax
from jax.experimental import pallas as pl
from jax.experimental.pallas import tpu as pltpu
from jax.sharding import PartitionSpec as P

QUERY_HEADS = 64
KEY_VALUE_HEADS = 8
HEAD_WIDTH = 128
LANES = 128
GROUP = QUERY_HEADS // KEY_VALUE_HEADS
OUT_WIDTH = QUERY_HEADS * HEAD_WIDTH

BLOCK_ROWS = QUERY_HEADS + 8

SCORE_SCALE = HEAD_WIDTH ** (-0.5)
EXP2_SCALE = SCORE_SCALE * math.log2(math.e)

STAGE_BYTES = 16 * 1024 * 1024
MERGE_VMEM = 16 * 1024 * 1024
ATTEND_VMEM = 44 * 1024 * 1024
UNROLLED_STEPS = 8
BESIDE_STEP = 4


def columns_at(head):
    if isinstance(head, int):
        return slice(head * HEAD_WIDTH, (head + 1) * HEAD_WIDTH)
    return pl.ds(pl.multiple_of(head * HEAD_WIDTH, HEAD_WIDTH), HEAD_WIDTH)


def iota(shape, dimension):
    return lax.broadcasted_iota(jnp.int32, shape, dimension)


def heads_down(row):
    sublane = iota((GROUP, HEAD_WIDTH), 0)
    tiles = []
    for head in range(KEY_VALUE_HEADS):
        tile = jnp.zeros((GROUP, HEAD_WIDTH), jnp.float32)
        for i in range(GROUP):
            tile = jnp.where(sublane == i, row[:, columns_at(head * GROUP + i)], tile)
        tiles.append(tile)
    return jnp.concatenate(tiles, axis=0)


def spread_heads(row):
    return jnp.concatenate(
        [
            jnp.broadcast_to(row[:, columns_at(head)], (GROUP, HEAD_WIDTH))
            for head in range(KEY_VALUE_HEADS)
        ],
        axis=0,
    )


def pack_lse(lse):
    shape = (QUERY_HEADS, LANES)
    own = (iota(shape, 1) & (QUERY_HEADS - 1)) == iota(shape, 0)
    along = jnp.sum(jnp.where(own, lse, 0.0), axis=0, keepdims=True)
    high = along.astype(jnp.bfloat16).astype(jnp.float32)
    rest = along - high
    middle = rest.astype(jnp.bfloat16).astype(jnp.float32)
    low = rest - middle
    tile = (8, LANES)
    first = jnp.where(iota(tile, 1) < QUERY_HEADS, high, middle)
    return jnp.where(iota(tile, 0) < 4, first, low).astype(jnp.bfloat16)


def unpack_lse(tile):
    tile = tile.astype(jnp.float32)
    first = tile[0:1]
    along = first + pltpu.roll(first, QUERY_HEADS, 1) + tile[4:5]
    shape = (QUERY_HEADS, LANES)
    chosen = jnp.where(iota(shape, 1) == iota(shape, 0), along, 0.0)
    return jnp.sum(chosen, axis=1, keepdims=True)


def exchange_steps(slots):
    return [(slots >> (i + 1)) | 1 for i in range(slots.bit_length() - 1)]


def slot_of_row(rows, me, slots):
    distance = rows ^ me
    slot, parity = 0, 0
    for i, step in enumerate(exchange_steps(slots)):
        bit = distance if step == 1 else lax.shift_right_logical(distance, step.bit_length() - 1)
        bit = (bit ^ parity if step == 1 else bit) & 1
        parity = parity ^ bit
        slot = slot + bit * (1 << i)
    return slot


def for_rows(count, body):
    if count <= 16:
        for row in range(count):
            body(row)
    else:

        def one(row, carry):
            body(row)
            return carry

        lax.fori_loop(0, count, one, 0)


def stage_kernel(
    home_hbm, lengths_hbm, query_hbm, fresh_hbm, prefix_hbm, suffix_hbm,
    query_ref, fresh_ref, where_ref, home_buf, lengths_buf, query_buf, sems, *, slots
):
    pairs = (
        (home_hbm, home_buf),
        (lengths_hbm, lengths_buf),
        (query_hbm, query_buf),
        (fresh_hbm, fresh_ref),
    )
    copies = [
        pltpu.make_async_copy(source, target, sems.at[i])
        for i, (source, target) in enumerate(pairs)
    ]
    for copy in copies:
        copy.start()
    for copy in copies:
        copy.wait()
    me = lax.axis_index("blk")
    here = home_buf[...] == me
    row_ids = iota(here.shape, 1)

    def pick(values):
        chosen = jnp.where(here, values, 0).astype(jnp.float32)
        return jnp.sum(chosen, axis=1, keepdims=True).astype(jnp.int32)

    slot = pick(slot_of_row(row_ids, me, slots))
    where_ref[...] = jnp.where(iota(where_ref.shape, 1) == 0, slot, pick(lengths_buf[...]))
    query_ref[0] = heads_down(query_buf[...].astype(jnp.float32)).astype(jnp.bfloat16)


def first_join_kernel(query_ref, landed_ref, out_ref):
    out_ref[0] = query_ref[0]
    out_ref[1] = heads_down(landed_ref[...].astype(jnp.float32)).astype(jnp.bfloat16)


def join_kernel(*refs):
    rows = refs[0].shape[0]
    for i, ref in enumerate(refs[:-1]):
        refs[-1][i * rows : (i + 1) * rows] = ref[...]


def contract(left, right):
    return lax.dot_general(left, right, (((1,), (1,)), ((), ())), preferred_element_type=jnp.float32)


def pair_columns(pair):
    if isinstance(pair, int):
        return slice(pair * 2 * HEAD_WIDTH, (pair + 1) * 2 * HEAD_WIDTH)
    return pl.ds(pl.multiple_of(pair * 2 * HEAD_WIDTH, 2 * HEAD_WIDTH), 2 * HEAD_WIDTH)


def group_rows(head):
    if isinstance(head, int):
        return slice(head * GROUP, (head + 1) * GROUP)
    return pl.ds(pl.multiple_of(head * GROUP, GROUP), GROUP)


def diagonal(first, second):
    first = jnp.concatenate([first, jnp.zeros_like(first)], axis=1)
    second = jnp.concatenate([jnp.zeros_like(second), second], axis=1)
    return jnp.concatenate([first, second], axis=0).astype(jnp.bfloat16)


def step_rows(slots):
    return 2 * GROUP * min(slots, LANES // GROUP)


def attend_prefix(
    query_ref,
    prefix_ref,
    out_ref,
    lse_ref,
    score_buf,
    weight_buf,
    inverse_buf,
    first_pair=0,
    pairs=KEY_VALUE_HEADS // 2,
    beside=None,
):
    slots = query_ref.shape[0]
    rows = step_rows(slots)
    side = rows // 2
    block = side // GROUP
    blocks = slots // block
    steps = pairs * blocks
    prefix_length = prefix_ref.shape[1]
    chunk_rows = 2 * GROUP
    chunks = rows // chunk_rows
    score_chunks = 4
    chunk_keys = prefix_length // score_chunks

    def block_rows(step):
        start = step % blocks * block
        return slice(start, start + block) if isinstance(start, int) else pl.ds(start, block)

    def score(step, buffer, chunk):
        pair = first_pair + step // blocks
        queries = diagonal(
            *(
                query_ref[block_rows(step), group_rows(2 * pair + member), :]
                .astype(jnp.float32)
                .reshape(side, HEAD_WIDTH)
                for member in range(2)
            )
        )
        keys = slice(chunk * chunk_keys, (chunk + 1) * chunk_keys)
        score_buf[buffer, :, keys] = contract(queries, prefix_ref[0, keys, pair_columns(pair)])

    def weigh(step, buffer, chunk):
        span = slice(chunk * chunk_rows, (chunk + 1) * chunk_rows)
        scores = score_buf[buffer, span, :]
        peak = jnp.max(scores, axis=1, keepdims=True)
        weights = jnp.exp2(scores * EXP2_SCALE - peak * EXP2_SCALE)
        total = jnp.sum(weights, axis=1, keepdims=True)
        weight_buf[buffer, span, :] = weights.astype(jnp.bfloat16)
        inverse_buf[buffer, span, :] = jnp.broadcast_to(1.0 / total, (chunk_rows, LANES))
        lse = jnp.broadcast_to(peak * SCORE_SCALE + jnp.log(total), (chunk_rows, LANES))
        head = (first_pair + step // blocks) * 2 + chunk * chunk_rows // side
        slot = step % blocks * block + chunk * chunk_rows % side // GROUP
        lse_ref[slot, group_rows(head), :] = lse[:GROUP]
        lse_ref[slot + 1, group_rows(head), :] = lse[GROUP:]

    def gather_values(step, buffer):
        pair = first_pair + step // blocks
        accum = jnp.dot(
            weight_buf[buffer],
            prefix_ref[1, :, pair_columns(pair)],
            preferred_element_type=jnp.float32,
        )
        for member in range(2):
            span = slice(member * side, (member + 1) * side)
            normed = accum[span, columns_at(member)] * inverse_buf[buffer, span, :]
            out_ref[block_rows(step), group_rows(2 * pair + member), :] = normed.reshape(
                block, GROUP, HEAD_WIDTH
            )

    if steps <= UNROLLED_STEPS:
        for step in range(steps + 2):
            if beside and step == BESIDE_STEP:
                beside()
            for chunk in range(chunks):
                if step < steps and chunk % (chunks // score_chunks) == 0:
                    score(step, step % 2, chunk // (chunks // score_chunks))
                if 1 <= step <= steps:
                    weigh(step - 1, (step - 1) % 2, chunk)
            if step >= 2:
                gather_values(step - 2, step % 2)
    else:
        if beside:
            beside()

        def one_step(step, carry):
            for chunk in range(score_chunks):
                score(step, 0, chunk)
            for chunk in range(chunks):
                weigh(step, 0, chunk)
            gather_values(step, 0)
            return carry

        lax.fori_loop(0, steps, one_step, 0)


def attend_suffix(query, live, suffix_ref):
    suffix_length = suffix_ref.shape[2]
    pairs = range(KEY_VALUE_HEADS // 2)
    scores = jnp.concatenate(
        [
            contract(
                diagonal(query[group_rows(2 * pair)], query[group_rows(2 * pair + 1)]),
                suffix_ref[0, 0, :, pair_columns(pair)],
            )
            for pair in pairs
        ],
        axis=0,
    )
    scores = jnp.where(iota((1, suffix_length), 1) < live, scores, -jnp.inf)
    peak = jnp.max(scores, axis=1, keepdims=True)
    weights = jnp.exp2((scores - peak) * EXP2_SCALE)
    total = jnp.sum(weights, axis=1, keepdims=True)
    weights = weights.astype(jnp.bfloat16)
    accum = []
    for pair in pairs:
        both = jnp.dot(
            weights[2 * pair * GROUP : 2 * (pair + 1) * GROUP],
            suffix_ref[0, 1, :, pair_columns(pair)],
            preferred_element_type=jnp.float32,
        )
        accum += [both[:GROUP, :HEAD_WIDTH], both[GROUP:, HEAD_WIDTH:]]
    value = jnp.concatenate(accum, axis=0) * (1.0 / total)
    lse = peak * SCORE_SCALE + jnp.log(total)
    return value, jnp.broadcast_to(lse, (QUERY_HEADS, LANES))


def suffix_place(where_ref):
    places = where_ref[...].astype(jnp.float32)
    return jnp.sum(jnp.where(iota(places.shape, 1) == 0, places, 0.0)).astype(jnp.int32)


def far_kernel(
    where_ref,
    near_ref,
    far_ref,
    prefix_ref,
    suffix_ref,
    early_lse_ref,
    send_ref,
    part_ref,
    part_lse_ref,
    out_buf,
    lse_buf,
    *buffers,
):
    half = far_ref.shape[0]
    place = suffix_place(where_ref)
    is_far = place >= half
    near_row = jnp.minimum(place, half - 1)
    far_row = jnp.maximum(place - half, 0)
    near_query = near_ref[near_row].astype(jnp.float32)
    far_query = far_ref[far_row].astype(jnp.float32)
    query = jnp.where(is_far, far_query, near_query)

    def suffix():
        part_ref[...], part_lse_ref[...] = attend_suffix(query, where_ref[:, 1:2], suffix_ref)

    attend_prefix(far_ref, prefix_ref, out_buf, lse_buf, *buffers, beside=suffix)

    lse = part_lse_ref[...]
    out_buf[far_row], lse_buf[far_row] = merge_parts(
        [lse_buf[far_row], jnp.where(is_far, lse, -jnp.inf)], [out_buf[far_row], part_ref[...]]
    )
    part_lse_ref[...] = jnp.where(is_far, -jnp.inf, lse)

    def write(row):
        send_ref[row, :QUERY_HEADS] = out_buf[row].astype(jnp.bfloat16)
        send_ref[row, QUERY_HEADS:] = pack_lse(lse_buf[row])

    for_rows(half, write)


EARLY_PAIRS = KEY_VALUE_HEADS // 4
EARLY_HEADS = EARLY_PAIRS * 2 * GROUP


def near_kernel(near_ref, prefix_ref, out_ref, lse_ref, *buffers):
    attend_prefix(near_ref, prefix_ref, out_ref, lse_ref, *buffers, pairs=EARLY_PAIRS)


def rest_kernel(
    where_ref,
    near_ref,
    prefix_ref,
    part_ref,
    part_lse_ref,
    early_ref,
    early_lse_ref,
    keep_ref,
    keep_lse_ref,
    *buffers,
):
    row = jnp.minimum(suffix_place(where_ref), near_ref.shape[0] - 1)
    keep_ref[:, :EARLY_HEADS] = early_ref[...]
    keep_lse_ref[:, :EARLY_HEADS] = early_lse_ref[...]
    attend_prefix(
        near_ref,
        prefix_ref,
        keep_ref,
        keep_lse_ref,
        *buffers,
        first_pair=EARLY_PAIRS,
        pairs=KEY_VALUE_HEADS // 2 - EARLY_PAIRS,
    )
    keep_ref[row], keep_lse_ref[row] = merge_parts(
        [keep_lse_ref[row], part_lse_ref[...]], [keep_ref[row], part_ref[...]]
    )


def merge_parts(lses, values):
    highest = functools.reduce(jnp.maximum, lses)
    weights = [jnp.exp(lse - highest) for lse in lses]
    total = functools.reduce(jnp.add, weights)
    merged = functools.reduce(jnp.add, [w * value for w, value in zip(weights, values)])
    return merged * (1.0 / total), highest + jnp.log(total)


def fresh_kernel(query_ref, fresh_ref, keep_ref, keep_lse_ref, out_ref, out_lse_ref):
    key = spread_heads(fresh_ref[0, 0:1, :].astype(jnp.float32))
    value = spread_heads(fresh_ref[0, 1:2, :].astype(jnp.float32))
    products = query_ref[0].astype(jnp.float32) * key
    lse = jnp.sum(products, axis=1, keepdims=True) * SCORE_SCALE
    out_ref[0], out_lse_ref[0] = merge_parts([keep_lse_ref[0], lse], [keep_ref[0], value])


def merge_kernel(keep_ref, keep_lse_ref, *refs, rows, parts, landings):
    landed_refs, out_refs = refs[:landings], refs[landings:]
    size = rows // parts

    def merge(row):
        lses = [keep_lse_ref[row]] + [unpack_lse(ref[row, QUERY_HEADS:]) for ref in landed_refs]
        values = [keep_ref[row]] + [
            ref[row, :QUERY_HEADS].astype(jnp.float32) for ref in landed_refs
        ]
        return merge_parts(lses, values)

    if parts == 1:
        merged, _ = merge(0)
        for c in range(QUERY_HEADS):
            out_refs[0][:, columns_at(c)] = merged[c : c + 1].astype(jnp.bfloat16)
        return

    def keep(row):
        out_refs[0][row], out_refs[1][row] = merge(row)

    for_rows(size, keep)
    for i in range(1, parts):

        def send(row):
            merged, lse = merge(i * size + row)
            out_refs[1 + i][row, :QUERY_HEADS] = merged.astype(jnp.bfloat16)
            out_refs[1 + i][row, QUERY_HEADS:] = pack_lse(lse)

        for_rows(size, send)


def partial_shapes(rows):
    return (
        jax.ShapeDtypeStruct((rows, QUERY_HEADS, HEAD_WIDTH), jnp.float32),
        jax.ShapeDtypeStruct((rows, QUERY_HEADS, LANES), jnp.float32),
        jax.ShapeDtypeStruct((rows, BLOCK_ROWS, HEAD_WIDTH), jnp.bfloat16),
    )


def per_device(queries, prefix_key_value, suffix_key_value, fresh_key_value, lengths, home):
    slots = lax.axis_size("blk")
    bits = slots.bit_length() - 1
    assert queries.shape[0] == 1 and slots == 1 << bits and slots > 1
    vmem = pl.BlockSpec(memory_space=pltpu.VMEM)
    steps = exchange_steps(slots)

    def swap(array, step):
        return lax.ppermute(array, "blk", [(i, i ^ step) for i in range(slots)])

    def in_vmem(*arrays):
        return [pltpu.with_memory_space_constraint(array, pltpu.VMEM) for array in arrays]

    def join(kernel, rows, *arrays):
        return pl.pallas_call(
            kernel,
            out_shape=jax.ShapeDtypeStruct((rows, QUERY_HEADS, HEAD_WIDTH), jnp.bfloat16),
            in_specs=[vmem] * len(arrays),
            out_specs=vmem,
            compiler_params=pltpu.CompilerParams(vmem_limit_bytes=MERGE_VMEM),
            name="join",
        )(*in_vmem(*arrays))

    phases = [[step] for step in steps]
    if bits > 3:
        phases = phases[:-3] + [steps[-3:-1]] + phases[-1:]

    def partners(phase):
        return phase if len(phase) == 1 else [phase[0], phase[1], phase[0] ^ phase[1]]

    def exchange(arrays, distances):
        order = sorted(range(len(distances)), key=lambda i: distances[i])
        landed = {i: swap(arrays[i], distances[i]) for i in order}
        return [landed[i] for i in range(len(distances))]

    landed = swap(queries, steps[0])
    query, fresh, where = pl.pallas_call(
        functools.partial(stage_kernel, slots=slots),
        out_shape=(
            pltpu.VMEM((1, QUERY_HEADS, HEAD_WIDTH), jnp.bfloat16),
            pltpu.VMEM(fresh_key_value.shape, jnp.bfloat16),
            pltpu.VMEM((1, LANES), jnp.int32),
        ),
        in_specs=[pl.BlockSpec(memory_space=pltpu.HBM)] * 6,
        out_specs=(vmem,) * 3,
        scratch_shapes=[
            pltpu.VMEM((1, slots), jnp.int32),
            pltpu.VMEM((1, slots), jnp.int32),
            pltpu.VMEM(queries.shape, jnp.bfloat16),
            pltpu.SemaphoreType.DMA((4,)),
        ],
        compiler_params=pltpu.CompilerParams(vmem_limit_bytes=MERGE_VMEM),
        cost_estimate=pl.CostEstimate(flops=0, bytes_accessed=STAGE_BYTES, transcendentals=0),
        name="stage",
    )(
        *(
            pltpu.with_memory_space_constraint(array, pltpu.HBM)
            for array in (
                home.reshape(1, slots),
                lengths.reshape(1, slots),
                queries,
                fresh_key_value,
                prefix_key_value,
                suffix_key_value,
            )
        )
    )
    gathered = join(first_join_kernel, 2, query, landed)
    for phase in phases[1:-1]:
        landed = exchange([gathered] * len(partners(phase)), partners(phase))
        gathered = join(join_kernel, gathered.shape[0] << len(phase), gathered, *landed)

    half = slots // 2
    rows, prefix_length = step_rows(half), prefix_key_value.shape[1]
    shapes = partial_shapes(half)
    part_shape = jax.ShapeDtypeStruct((QUERY_HEADS, LANES), jnp.float32)
    early_shape = jax.ShapeDtypeStruct((half, EARLY_HEADS, LANES), jnp.float32)
    buffers = [
        pltpu.VMEM((2, rows, prefix_length), jnp.float32),
        pltpu.VMEM((2, rows, prefix_length), jnp.bfloat16),
        pltpu.VMEM((2, rows, LANES), jnp.float32),
    ]

    def attend(kernel, name, out_shape, scratch, *arrays):
        return pl.pallas_call(
            kernel,
            out_shape=out_shape,
            in_specs=[vmem] * len(arrays),
            out_specs=(vmem,) * len(out_shape),
            scratch_shapes=scratch + buffers,
            compiler_params=pltpu.CompilerParams(vmem_limit_bytes=ATTEND_VMEM),
            cost_estimate=pl.CostEstimate(
                flops=0, bytes_accessed=STAGE_BYTES // 4, transcendentals=0
            ),
            name=name,
        )(*in_vmem(*arrays))

    (other,) = exchange([gathered], phases[-1])
    early, early_lse = attend(
        near_kernel, "near", (early_shape, early_shape), [], gathered, prefix_key_value
    )
    send, part, part_lse = attend(
        far_kernel,
        "far",
        (shapes[2], part_shape, part_shape),
        [pltpu.VMEM(shape.shape, shape.dtype) for shape in shapes[:2]],
        where,
        gathered,
        other,
        prefix_key_value,
        suffix_key_value,
        early_lse,
    )
    (landed,) = exchange([send], phases[-1])
    keep, keep_lse = attend(
        rest_kernel,
        "rest",
        shapes[:2],
        [],
        where,
        gathered,
        prefix_key_value,
        part,
        part_lse,
        early,
        early_lse,
    )

    rows = half
    landed = [landed]
    for i, phase in enumerate(phases[::-1]):
        if i > 0:
            landed = exchange(sends, partners(phase))
        if i == len(phases) - 1:
            parts, shapes = 1, (jax.ShapeDtypeStruct((1, OUT_WIDTH), jnp.bfloat16),)
            keep, keep_lse = pl.pallas_call(
                fresh_kernel,
                out_shape=partial_shapes(1)[:2],
                in_specs=[vmem] * 4,
                out_specs=(vmem,) * 2,
                compiler_params=pltpu.CompilerParams(vmem_limit_bytes=MERGE_VMEM),
                cost_estimate=pl.CostEstimate(
                    flops=0, bytes_accessed=STAGE_BYTES // 8, transcendentals=0
                ),
                name="fresh",
            )(*in_vmem(query, fresh, keep, keep_lse))
        else:
            parts = 1 << len(phases[-2 - i])
            shapes = partial_shapes(rows // parts)
            shapes = shapes[:2] + shapes[2:] * (parts - 1)
        merged = pl.pallas_call(
            functools.partial(merge_kernel, rows=rows, parts=parts, landings=len(landed)),
            out_shape=shapes,
            in_specs=[vmem] * (2 + len(landed)),
            out_specs=(vmem,) * len(shapes),
            compiler_params=pltpu.CompilerParams(vmem_limit_bytes=MERGE_VMEM),
            name="merge",
        )(keep, keep_lse, *landed[::-1])
        if parts > 1:
            keep, keep_lse, *sends = merged
            rows = rows // parts
    return merged[0]


def solution(mesh):
    placed = (
        P(("groups", "blk"), None),
        P(None, ("groups", "blk"), None),
        P(("groups", "blk"), None, None, None),
        P(("groups", "blk"), None, None),
        P("groups"),
        P("groups"),
    )
    return jax.shard_map(
        per_device,
        mesh=mesh,
        in_specs=placed,
        out_specs=P(("groups", "blk"), None),
        check_vma=False,
    )
```

```python
import functools
import math

import jax
import jax.numpy as jnp
from jax import lax
from jax.experimental import pallas as pl
from jax.experimental.pallas import tpu as pltpu
from jax.sharding import PartitionSpec as P

QUERY_HEADS = 64
KEY_VALUE_HEADS = 8
HEAD_WIDTH = 128
LANES = 128
GROUP = QUERY_HEADS // KEY_VALUE_HEADS
OUT_WIDTH = QUERY_HEADS * HEAD_WIDTH

BLOCK_ROWS = QUERY_HEADS + 8

SCORE_SCALE = HEAD_WIDTH ** (-0.5)
EXP2_SCALE = SCORE_SCALE * math.log2(math.e)

STAGE_BYTES = 16 * 1024 * 1024
MERGE_VMEM = 16 * 1024 * 1024
ATTEND_VMEM = 44 * 1024 * 1024
UNROLLED_STEPS = 8
BESIDE_STEP = 4


def columns_at(head):
    if isinstance(head, int):
        return slice(head * HEAD_WIDTH, (head + 1) * HEAD_WIDTH)
    return pl.ds(pl.multiple_of(head * HEAD_WIDTH, HEAD_WIDTH), HEAD_WIDTH)


def iota(shape, dimension):
    return lax.broadcasted_iota(jnp.int32, shape, dimension)


def heads_down(row):
    sublane = iota((GROUP, HEAD_WIDTH), 0)
    tiles = []
    for head in range(KEY_VALUE_HEADS):
        tile = jnp.zeros((GROUP, HEAD_WIDTH), jnp.float32)
        for i in range(GROUP):
            tile = jnp.where(sublane == i, row[:, columns_at(head * GROUP + i)], tile)
        tiles.append(tile)
    return jnp.concatenate(tiles, axis=0)


def spread_heads(row):
    return jnp.concatenate(
        [
            jnp.broadcast_to(row[:, columns_at(head)], (GROUP, HEAD_WIDTH))
            for head in range(KEY_VALUE_HEADS)
        ],
        axis=0,
    )


def pack_lse(lse):
    shape = (QUERY_HEADS, LANES)
    own = (iota(shape, 1) & (QUERY_HEADS - 1)) == iota(shape, 0)
    along = jnp.sum(jnp.where(own, lse, 0.0), axis=0, keepdims=True)
    high = along.astype(jnp.bfloat16).astype(jnp.float32)
    rest = along - high
    middle = rest.astype(jnp.bfloat16).astype(jnp.float32)
    low = rest - middle
    tile = (8, LANES)
    first = jnp.where(iota(tile, 1) < QUERY_HEADS, high, middle)
    return jnp.where(iota(tile, 0) < 4, first, low).astype(jnp.bfloat16)


def unpack_lse(tile):
    tile = tile.astype(jnp.float32)
    first = tile[0:1]
    along = first + pltpu.roll(first, QUERY_HEADS, 1) + tile[4:5]
    shape = (QUERY_HEADS, LANES)
    chosen = jnp.where(iota(shape, 1) == iota(shape, 0), along, 0.0)
    return jnp.sum(chosen, axis=1, keepdims=True)


def exchange_phases(slots):
    steps = [(slots >> (i + 1)) | 1 for i in range(slots.bit_length() - 1)]
    phases = [[step] for step in steps]
    if len(steps) > 3:
        phases = phases[:-3] + [steps[-3:-1]] + phases[-1:]
    return phases


def partners(phase):
    return phase if len(phase) == 1 else [phase[0], phase[1], phase[0] | phase[1]]


def slot_of_row(rows, me, slots):
    distance = rows ^ me
    slot, other_core, place = 0, distance & 1, 0
    for phase in exchange_phases(slots)[:-1]:
        crossed = 0
        for step in phase:
            bit = lax.shift_right_logical(distance, step.bit_length() - 1) & 1
            slot = slot + bit * (1 << place)
            crossed = crossed | bit
            place += 1
        other_core = other_core ^ crossed
    return slot + other_core * (1 << place)


def for_rows(count, body):
    if count <= 16:
        for row in range(count):
            body(row)
    else:

        def one(row, carry):
            body(row)
            return carry

        lax.fori_loop(0, count, one, 0)


def stage_kernel(
    home_hbm, lengths_hbm, query_hbm, fresh_hbm, prefix_hbm, suffix_hbm,
    query_ref, fresh_ref, where_ref, home_buf, lengths_buf, query_buf, sems, *, slots
):
    pairs = (
        (home_hbm, home_buf),
        (lengths_hbm, lengths_buf),
        (query_hbm, query_buf),
        (fresh_hbm, fresh_ref),
    )
    copies = [
        pltpu.make_async_copy(source, target, sems.at[i])
        for i, (source, target) in enumerate(pairs)
    ]
    for copy in copies:
        copy.start()
    for copy in copies:
        copy.wait()
    me = lax.axis_index("blk")
    here = home_buf[...] == me
    row_ids = iota(here.shape, 1)

    def pick(values):
        chosen = jnp.where(here, values, 0).astype(jnp.float32)
        return jnp.sum(chosen, axis=1, keepdims=True).astype(jnp.int32)

    slot = pick(slot_of_row(row_ids, me, slots))
    where_ref[...] = jnp.where(iota(where_ref.shape, 1) == 0, slot, pick(lengths_buf[...]))
    query_ref[0] = heads_down(query_buf[...].astype(jnp.float32)).astype(jnp.bfloat16)


def first_join_kernel(query_ref, landed_ref, out_ref):
    out_ref[0] = query_ref[0]
    out_ref[1] = heads_down(landed_ref[...].astype(jnp.float32)).astype(jnp.bfloat16)


def join_kernel(*refs):
    rows = refs[0].shape[0]
    for i, ref in enumerate(refs[:-1]):
        refs[-1][i * rows : (i + 1) * rows] = ref[...]


def contract(left, right):
    return lax.dot_general(left, right, (((1,), (1,)), ((), ())), preferred_element_type=jnp.float32)


def pair_columns(pair):
    if isinstance(pair, int):
        return slice(pair * 2 * HEAD_WIDTH, (pair + 1) * 2 * HEAD_WIDTH)
    return pl.ds(pl.multiple_of(pair * 2 * HEAD_WIDTH, 2 * HEAD_WIDTH), 2 * HEAD_WIDTH)


def group_rows(head):
    if isinstance(head, int):
        return slice(head * GROUP, (head + 1) * GROUP)
    return pl.ds(pl.multiple_of(head * GROUP, GROUP), GROUP)


def diagonal(first, second):
    first = jnp.concatenate([first, jnp.zeros_like(first)], axis=1)
    second = jnp.concatenate([jnp.zeros_like(second), second], axis=1)
    return jnp.concatenate([first, second], axis=0).astype(jnp.bfloat16)


def step_rows(slots):
    return 2 * GROUP * min(slots, LANES // GROUP)


def attend_prefix(
    query_ref,
    prefix_ref,
    out_ref,
    lse_ref,
    score_buf,
    weight_buf,
    inverse_buf,
    first_pair=0,
    pairs=KEY_VALUE_HEADS // 2,
    beside=None,
):
    slots = query_ref.shape[0]
    rows = step_rows(slots)
    side = rows // 2
    block = side // GROUP
    blocks = slots // block
    steps = pairs * blocks
    prefix_length = prefix_ref.shape[1]
    chunk_rows = 2 * GROUP
    chunks = rows // chunk_rows
    score_chunks = 2
    chunk_keys = prefix_length // score_chunks

    def block_rows(step):
        start = step % blocks * block
        return slice(start, start + block) if isinstance(start, int) else pl.ds(start, block)

    def score(step, buffer, chunk):
        pair = first_pair + step // blocks
        queries = diagonal(
            *(
                query_ref[block_rows(step), group_rows(2 * pair + member), :]
                .astype(jnp.float32)
                .reshape(side, HEAD_WIDTH)
                for member in range(2)
            )
        )
        keys = slice(chunk * chunk_keys, (chunk + 1) * chunk_keys)
        score_buf[buffer, :, keys] = contract(queries, prefix_ref[0, keys, pair_columns(pair)])

    def weigh(step, buffer, chunk):
        span = slice(chunk * chunk_rows, (chunk + 1) * chunk_rows)
        scores = score_buf[buffer, span, :]
        peak = jnp.max(scores, axis=1, keepdims=True)
        weights = jnp.exp2(scores * EXP2_SCALE - peak * EXP2_SCALE)
        total = jnp.sum(weights, axis=1, keepdims=True)
        weight_buf[buffer, span, :] = weights.astype(jnp.bfloat16)
        inverse_buf[buffer, span, :] = jnp.broadcast_to(1.0 / total, (chunk_rows, LANES))
        lse = jnp.broadcast_to(peak * SCORE_SCALE + jnp.log(total), (chunk_rows, LANES))
        head = (first_pair + step // blocks) * 2 + chunk * chunk_rows // side
        slot = step % blocks * block + chunk * chunk_rows % side // GROUP
        lse_ref[slot, group_rows(head), :] = lse[:GROUP]
        lse_ref[slot + 1, group_rows(head), :] = lse[GROUP:]

    def gather_values(step, buffer):
        pair = first_pair + step // blocks
        accum = jnp.dot(
            weight_buf[buffer],
            prefix_ref[1, :, pair_columns(pair)],
            preferred_element_type=jnp.float32,
        )
        for member in range(2):
            span = slice(member * side, (member + 1) * side)
            normed = accum[span, columns_at(member)] * inverse_buf[buffer, span, :]
            out_ref[block_rows(step), group_rows(2 * pair + member), :] = normed.reshape(
                block, GROUP, HEAD_WIDTH
            )

    if steps <= UNROLLED_STEPS:
        for step in range(steps + 2):
            if beside and step == BESIDE_STEP:
                beside()
            for chunk in range(chunks):
                if step < steps and chunk % (chunks // score_chunks) == 0:
                    score(step, step % 2, chunk // (chunks // score_chunks))
                if 1 <= step <= steps:
                    weigh(step - 1, (step - 1) % 2, chunk)
            if step >= 2:
                gather_values(step - 2, step % 2)
    else:
        if beside:
            beside()

        def one_step(step, carry):
            for chunk in range(score_chunks):
                score(step, 0, chunk)
            for chunk in range(chunks):
                weigh(step, 0, chunk)
            gather_values(step, 0)
            return carry

        lax.fori_loop(0, steps, one_step, 0)


def attend_suffix(query, live, suffix_ref):
    suffix_length = suffix_ref.shape[2]
    pairs = range(KEY_VALUE_HEADS // 2)
    scores = jnp.concatenate(
        [
            contract(
                diagonal(query[group_rows(2 * pair)], query[group_rows(2 * pair + 1)]),
                suffix_ref[0, 0, :, pair_columns(pair)],
            )
            for pair in pairs
        ],
        axis=0,
    )
    scores = jnp.where(iota((1, suffix_length), 1) < live, scores, -jnp.inf)
    peak = jnp.max(scores, axis=1, keepdims=True)
    weights = jnp.exp2((scores - peak) * EXP2_SCALE)
    total = jnp.sum(weights, axis=1, keepdims=True)
    weights = weights.astype(jnp.bfloat16)
    accum = []
    for pair in pairs:
        both = jnp.dot(
            weights[2 * pair * GROUP : 2 * (pair + 1) * GROUP],
            suffix_ref[0, 1, :, pair_columns(pair)],
            preferred_element_type=jnp.float32,
        )
        accum += [both[:GROUP, :HEAD_WIDTH], both[GROUP:, HEAD_WIDTH:]]
    value = jnp.concatenate(accum, axis=0) * (1.0 / total)
    lse = peak * SCORE_SCALE + jnp.log(total)
    return value, jnp.broadcast_to(lse, (QUERY_HEADS, LANES))


def suffix_place(where_ref):
    places = where_ref[...].astype(jnp.float32)
    return jnp.sum(jnp.where(iota(places.shape, 1) == 0, places, 0.0)).astype(jnp.int32)


def far_kernel(
    where_ref,
    near_ref,
    far_ref,
    prefix_ref,
    suffix_ref,
    early_lse_ref,
    send_ref,
    part_ref,
    part_lse_ref,
    out_buf,
    lse_buf,
    *buffers,
):
    half = far_ref.shape[0]
    place = suffix_place(where_ref)
    is_far = place >= half
    near_row = jnp.minimum(place, half - 1)
    far_row = jnp.maximum(place - half, 0)
    near_query = near_ref[near_row].astype(jnp.float32)
    far_query = far_ref[far_row].astype(jnp.float32)
    query = jnp.where(is_far, far_query, near_query)

    def suffix():
        part_ref[...], part_lse_ref[...] = attend_suffix(query, where_ref[:, 1:2], suffix_ref)

    attend_prefix(far_ref, prefix_ref, out_buf, lse_buf, *buffers, beside=suffix)

    lse = part_lse_ref[...]
    out_buf[far_row], lse_buf[far_row] = merge_parts(
        [lse_buf[far_row], jnp.where(is_far, lse, -jnp.inf)], [out_buf[far_row], part_ref[...]]
    )
    part_lse_ref[...] = jnp.where(is_far, -jnp.inf, lse)

    def write(row):
        send_ref[row, :QUERY_HEADS] = out_buf[row].astype(jnp.bfloat16)
        send_ref[row, QUERY_HEADS:] = pack_lse(lse_buf[row])

    for_rows(half, write)


EARLY_PAIRS = KEY_VALUE_HEADS // 4
EARLY_HEADS = EARLY_PAIRS * 2 * GROUP


def near_kernel(near_ref, prefix_ref, out_ref, lse_ref, *buffers):
    attend_prefix(near_ref, prefix_ref, out_ref, lse_ref, *buffers, pairs=EARLY_PAIRS)


def rest_kernel(
    where_ref,
    near_ref,
    prefix_ref,
    part_ref,
    part_lse_ref,
    early_ref,
    early_lse_ref,
    keep_ref,
    keep_lse_ref,
    *buffers,
):
    row = jnp.minimum(suffix_place(where_ref), near_ref.shape[0] - 1)
    keep_ref[:, :EARLY_HEADS] = early_ref[...]
    keep_lse_ref[:, :EARLY_HEADS] = early_lse_ref[...]
    attend_prefix(
        near_ref,
        prefix_ref,
        keep_ref,
        keep_lse_ref,
        *buffers,
        first_pair=EARLY_PAIRS,
        pairs=KEY_VALUE_HEADS // 2 - EARLY_PAIRS,
    )
    keep_ref[row], keep_lse_ref[row] = merge_parts(
        [keep_lse_ref[row], part_lse_ref[...]], [keep_ref[row], part_ref[...]]
    )


def merge_parts(lses, values):
    highest = functools.reduce(jnp.maximum, lses)
    weights = [jnp.exp(lse - highest) for lse in lses]
    total = functools.reduce(jnp.add, weights)
    merged = functools.reduce(jnp.add, [w * value for w, value in zip(weights, values)])
    return merged * (1.0 / total), highest + jnp.log(total)


def fresh_kernel(query_ref, fresh_ref, keep_ref, keep_lse_ref, out_ref, out_lse_ref):
    key = spread_heads(fresh_ref[0, 0:1, :].astype(jnp.float32))
    value = spread_heads(fresh_ref[0, 1:2, :].astype(jnp.float32))
    products = query_ref[0].astype(jnp.float32) * key
    lse = jnp.sum(products, axis=1, keepdims=True) * SCORE_SCALE
    out_ref[0], out_lse_ref[0] = merge_parts([keep_lse_ref[0], lse], [keep_ref[0], value])


def merge_kernel(keep_ref, keep_lse_ref, *refs, rows, parts, landings):
    landed_refs, out_refs = refs[:landings], refs[landings:]
    size = rows // parts

    def merge(row):
        lses = [keep_lse_ref[row]] + [unpack_lse(ref[row, QUERY_HEADS:]) for ref in landed_refs]
        values = [keep_ref[row]] + [
            ref[row, :QUERY_HEADS].astype(jnp.float32) for ref in landed_refs
        ]
        return merge_parts(lses, values)

    if parts == 1:
        merged, _ = merge(0)
        for c in range(QUERY_HEADS):
            out_refs[0][:, columns_at(c)] = merged[c : c + 1].astype(jnp.bfloat16)
        return

    def keep(row):
        out_refs[0][row], out_refs[1][row] = merge(row)

    for_rows(size, keep)
    for i in range(1, parts):

        def send(row):
            merged, lse = merge(i * size + row)
            out_refs[1 + i][row, :QUERY_HEADS] = merged.astype(jnp.bfloat16)
            out_refs[1 + i][row, QUERY_HEADS:] = pack_lse(lse)

        for_rows(size, send)


def partial_shapes(rows):
    return (
        jax.ShapeDtypeStruct((rows, QUERY_HEADS, HEAD_WIDTH), jnp.float32),
        jax.ShapeDtypeStruct((rows, QUERY_HEADS, LANES), jnp.float32),
        jax.ShapeDtypeStruct((rows, BLOCK_ROWS, HEAD_WIDTH), jnp.bfloat16),
    )


def per_device(queries, prefix_key_value, suffix_key_value, fresh_key_value, lengths, home):
    slots = lax.axis_size("blk")
    bits = slots.bit_length() - 1
    assert queries.shape[0] == 1 and slots == 1 << bits and slots > 1
    vmem = pl.BlockSpec(memory_space=pltpu.VMEM)
    phases = exchange_phases(slots)

    def swap(array, step):
        return lax.ppermute(array, "blk", [(i, i ^ step) for i in range(slots)])

    def in_vmem(*arrays):
        return [pltpu.with_memory_space_constraint(array, pltpu.VMEM) for array in arrays]

    def join(kernel, rows, *arrays):
        return pl.pallas_call(
            kernel,
            out_shape=jax.ShapeDtypeStruct((rows, QUERY_HEADS, HEAD_WIDTH), jnp.bfloat16),
            in_specs=[vmem] * len(arrays),
            out_specs=vmem,
            compiler_params=pltpu.CompilerParams(vmem_limit_bytes=MERGE_VMEM),
            name="join",
        )(*in_vmem(*arrays))

    def exchange(arrays, distances):
        order = sorted(range(len(distances)), key=lambda i: distances[i])
        landed = {i: swap(arrays[i], distances[i]) for i in order}
        return [landed[i] for i in range(len(distances))]

    landed = swap(queries, phases[0][0])
    query, fresh, where = pl.pallas_call(
        functools.partial(stage_kernel, slots=slots),
        out_shape=(
            pltpu.VMEM((1, QUERY_HEADS, HEAD_WIDTH), jnp.bfloat16),
            pltpu.VMEM(fresh_key_value.shape, jnp.bfloat16),
            pltpu.VMEM((1, LANES), jnp.int32),
        ),
        in_specs=[pl.BlockSpec(memory_space=pltpu.HBM)] * 6,
        out_specs=(vmem,) * 3,
        scratch_shapes=[
            pltpu.VMEM((1, slots), jnp.int32),
            pltpu.VMEM((1, slots), jnp.int32),
            pltpu.VMEM(queries.shape, jnp.bfloat16),
            pltpu.SemaphoreType.DMA((4,)),
        ],
        compiler_params=pltpu.CompilerParams(vmem_limit_bytes=MERGE_VMEM),
        cost_estimate=pl.CostEstimate(flops=0, bytes_accessed=STAGE_BYTES, transcendentals=0),
        name="stage",
    )(
        *(
            pltpu.with_memory_space_constraint(array, pltpu.HBM)
            for array in (
                home.reshape(1, slots),
                lengths.reshape(1, slots),
                queries,
                fresh_key_value,
                prefix_key_value,
                suffix_key_value,
            )
        )
    )
    gathered = join(first_join_kernel, 2, query, landed)
    for phase in phases[1:-1]:
        landed = exchange([gathered] * len(partners(phase)), partners(phase))
        gathered = join(join_kernel, gathered.shape[0] << len(phase), gathered, *landed)

    half = slots // 2
    rows, prefix_length = step_rows(half), prefix_key_value.shape[1]
    shapes = partial_shapes(half)
    part_shape = jax.ShapeDtypeStruct((QUERY_HEADS, LANES), jnp.float32)
    early_shape = jax.ShapeDtypeStruct((half, EARLY_HEADS, LANES), jnp.float32)
    buffers = [
        pltpu.VMEM((2, rows, prefix_length), jnp.float32),
        pltpu.VMEM((2, rows, prefix_length), jnp.bfloat16),
        pltpu.VMEM((2, rows, LANES), jnp.float32),
    ]

    def attend(kernel, name, out_shape, scratch, *arrays):
        return pl.pallas_call(
            kernel,
            out_shape=out_shape,
            in_specs=[vmem] * len(arrays),
            out_specs=(vmem,) * len(out_shape),
            scratch_shapes=scratch + buffers,
            compiler_params=pltpu.CompilerParams(vmem_limit_bytes=ATTEND_VMEM),
            cost_estimate=pl.CostEstimate(
                flops=0, bytes_accessed=STAGE_BYTES // 4, transcendentals=0
            ),
            name=name,
        )(*in_vmem(*arrays))

    (other,) = exchange([gathered], phases[-1])
    early, early_lse = attend(
        near_kernel, "near", (early_shape, early_shape), [], gathered, prefix_key_value
    )
    send, part, part_lse = attend(
        far_kernel,
        "far",
        (shapes[2], part_shape, part_shape),
        [pltpu.VMEM(shape.shape, shape.dtype) for shape in shapes[:2]],
        where,
        gathered,
        other,
        prefix_key_value,
        suffix_key_value,
        early_lse,
    )
    (landed,) = exchange([send], phases[-1])
    keep, keep_lse = attend(
        rest_kernel,
        "rest",
        shapes[:2],
        [],
        where,
        gathered,
        prefix_key_value,
        part,
        part_lse,
        early,
        early_lse,
    )

    rows = half
    landed = [landed]
    for i, phase in enumerate(phases[::-1]):
        if i > 0:
            landed = exchange(sends, partners(phase))
        if i == len(phases) - 1:
            parts, shapes = 1, (jax.ShapeDtypeStruct((1, OUT_WIDTH), jnp.bfloat16),)
            keep, keep_lse = pl.pallas_call(
                fresh_kernel,
                out_shape=partial_shapes(1)[:2],
                in_specs=[vmem] * 4,
                out_specs=(vmem,) * 2,
                compiler_params=pltpu.CompilerParams(vmem_limit_bytes=MERGE_VMEM),
                cost_estimate=pl.CostEstimate(
                    flops=0, bytes_accessed=STAGE_BYTES // 8, transcendentals=0
                ),
                name="fresh",
            )(*in_vmem(query, fresh, keep, keep_lse))
        else:
            parts = 1 << len(phases[-2 - i])
            shapes = partial_shapes(rows // parts)
            shapes = shapes[:2] + shapes[2:] * (parts - 1)
        merged = pl.pallas_call(
            functools.partial(merge_kernel, rows=rows, parts=parts, landings=len(landed)),
            out_shape=shapes,
            in_specs=[vmem] * (2 + len(landed)),
            out_specs=(vmem,) * len(shapes),
            compiler_params=pltpu.CompilerParams(vmem_limit_bytes=MERGE_VMEM),
            name="merge",
        )(keep, keep_lse, *landed[::-1])
        if parts > 1:
            keep, keep_lse, *sends = merged
            rows = rows // parts
    return merged[0]


def solution(mesh):
    placed = (
        P(("groups", "blk"), None),
        P(None, ("groups", "blk"), None),
        P(("groups", "blk"), None, None, None),
        P(("groups", "blk"), None, None),
        P("groups"),
        P("groups"),
    )
    return jax.shard_map(
        per_device,
        mesh=mesh,
        in_specs=placed,
        out_specs=P(("groups", "blk"), None),
        check_vma=False,
    )
```

```python
import functools
import math

import jax
import jax.numpy as jnp
from jax import lax
from jax.experimental import pallas as pl
from jax.experimental.pallas import tpu as pltpu
from jax.sharding import PartitionSpec as P

QUERY_HEADS = 64
KEY_VALUE_HEADS = 8
HEAD_WIDTH = 128
LANES = 128
GROUP = QUERY_HEADS // KEY_VALUE_HEADS
OUT_WIDTH = QUERY_HEADS * HEAD_WIDTH

BLOCK_ROWS = QUERY_HEADS + 8

SCORE_SCALE = HEAD_WIDTH ** (-0.5)
EXP2_SCALE = SCORE_SCALE * math.log2(math.e)

STAGE_BYTES = 16 * 1024 * 1024
MERGE_VMEM = 16 * 1024 * 1024
ATTEND_VMEM = 44 * 1024 * 1024
UNROLLED_STEPS = 8
BESIDE_STEP = 4


def columns_at(head):
    if isinstance(head, int):
        return slice(head * HEAD_WIDTH, (head + 1) * HEAD_WIDTH)
    return pl.ds(pl.multiple_of(head * HEAD_WIDTH, HEAD_WIDTH), HEAD_WIDTH)


def iota(shape, dimension):
    return lax.broadcasted_iota(jnp.int32, shape, dimension)


def heads_down(row):
    sublane = iota((GROUP, HEAD_WIDTH), 0)
    tiles = []
    for head in range(KEY_VALUE_HEADS):
        tile = jnp.zeros((GROUP, HEAD_WIDTH), jnp.float32)
        for i in range(GROUP):
            tile = jnp.where(sublane == i, row[:, columns_at(head * GROUP + i)], tile)
        tiles.append(tile)
    return jnp.concatenate(tiles, axis=0)


def spread_heads(row):
    return jnp.concatenate(
        [
            jnp.broadcast_to(row[:, columns_at(head)], (GROUP, HEAD_WIDTH))
            for head in range(KEY_VALUE_HEADS)
        ],
        axis=0,
    )


def pack_lse(lse):
    shape = (QUERY_HEADS, LANES)
    own = (iota(shape, 1) & (QUERY_HEADS - 1)) == iota(shape, 0)
    along = jnp.sum(jnp.where(own, lse, 0.0), axis=0, keepdims=True)
    high = along.astype(jnp.bfloat16).astype(jnp.float32)
    rest = along - high
    middle = rest.astype(jnp.bfloat16).astype(jnp.float32)
    low = rest - middle
    tile = (8, LANES)
    first = jnp.where(iota(tile, 1) < QUERY_HEADS, high, middle)
    return jnp.where(iota(tile, 0) < 4, first, low).astype(jnp.bfloat16)


def unpack_lse(tile):
    tile = tile.astype(jnp.float32)
    first = tile[0:1]
    along = first + pltpu.roll(first, QUERY_HEADS, 1) + tile[4:5]
    shape = (QUERY_HEADS, LANES)
    chosen = jnp.where(iota(shape, 1) == iota(shape, 0), along, 0.0)
    return jnp.sum(chosen, axis=1, keepdims=True)


def exchange_phases(slots):
    steps = [(slots >> (i + 1)) | 1 for i in range(slots.bit_length() - 1)]
    phases = [[step] for step in steps]
    if len(steps) > 3:
        phases = phases[:-3] + [steps[-3:-1]] + phases[-1:]
    return phases


def partners(phase):
    return phase if len(phase) == 1 else [phase[0], phase[1], phase[0] | phase[1]]


def slot_of_row(rows, me, slots):
    distance = rows ^ me
    slot, other_core, place = 0, distance & 1, 0
    for phase in exchange_phases(slots)[:-1]:
        crossed = 0
        for step in phase:
            bit = lax.shift_right_logical(distance, step.bit_length() - 1) & 1
            slot = slot + bit * (1 << place)
            crossed = crossed | bit
            place += 1
        other_core = other_core ^ crossed
    return slot + other_core * (1 << place)


def for_rows(count, body):
    if count <= 16:
        for row in range(count):
            body(row)
    else:

        def one(row, carry):
            body(row)
            return carry

        lax.fori_loop(0, count, one, 0)


def stage_kernel(
    home_hbm, lengths_hbm, query_hbm, fresh_hbm, prefix_hbm, suffix_hbm,
    query_ref, fresh_ref, where_ref, home_buf, lengths_buf, query_buf, sems, *, slots
):
    pairs = (
        (home_hbm, home_buf),
        (lengths_hbm, lengths_buf),
        (query_hbm, query_buf),
        (fresh_hbm, fresh_ref),
    )
    copies = [
        pltpu.make_async_copy(source, target, sems.at[i])
        for i, (source, target) in enumerate(pairs)
    ]
    for copy in copies:
        copy.start()
    for copy in copies:
        copy.wait()
    me = lax.axis_index("blk")
    here = home_buf[...] == me
    row_ids = iota(here.shape, 1)

    def pick(values):
        chosen = jnp.where(here, values, 0).astype(jnp.float32)
        return jnp.sum(chosen, axis=1, keepdims=True).astype(jnp.int32)

    slot = pick(slot_of_row(row_ids, me, slots))
    where_ref[...] = jnp.where(iota(where_ref.shape, 1) == 0, slot, pick(lengths_buf[...]))
    query_ref[0] = heads_down(query_buf[...].astype(jnp.float32)).astype(jnp.bfloat16)


def first_join_kernel(query_ref, landed_ref, out_ref):
    out_ref[0] = query_ref[0]
    out_ref[1] = heads_down(landed_ref[...].astype(jnp.float32)).astype(jnp.bfloat16)


def join_kernel(*refs):
    rows = refs[0].shape[0]
    for i, ref in enumerate(refs[:-1]):
        refs[-1][i * rows : (i + 1) * rows] = ref[...]


def contract(left, right):
    return lax.dot_general(left, right, (((1,), (1,)), ((), ())), preferred_element_type=jnp.float32)


def pair_columns(pair):
    if isinstance(pair, int):
        return slice(pair * 2 * HEAD_WIDTH, (pair + 1) * 2 * HEAD_WIDTH)
    return pl.ds(pl.multiple_of(pair * 2 * HEAD_WIDTH, 2 * HEAD_WIDTH), 2 * HEAD_WIDTH)


def group_rows(head):
    if isinstance(head, int):
        return slice(head * GROUP, (head + 1) * GROUP)
    return pl.ds(pl.multiple_of(head * GROUP, GROUP), GROUP)


def diagonal(first, second):
    first = jnp.concatenate([first, jnp.zeros_like(first)], axis=1)
    second = jnp.concatenate([jnp.zeros_like(second), second], axis=1)
    return jnp.concatenate([first, second], axis=0).astype(jnp.bfloat16)


def step_rows(slots):
    return 2 * GROUP * min(slots, LANES // GROUP)


def attend_prefix(
    query_ref,
    prefix_ref,
    out_ref,
    lse_ref,
    score_buf,
    weight_buf,
    inverse_buf,
    first_pair=0,
    pairs=KEY_VALUE_HEADS // 2,
    beside=None,
):
    slots = query_ref.shape[0]
    rows = step_rows(slots)
    side = rows // 2
    block = side // GROUP
    blocks = slots // block
    steps = pairs * blocks
    prefix_length = prefix_ref.shape[1]
    chunk_rows = 2 * GROUP
    chunks = rows // chunk_rows
    score_chunks = 2
    chunk_keys = prefix_length // score_chunks

    def block_rows(step):
        start = step % blocks * block
        return slice(start, start + block) if isinstance(start, int) else pl.ds(start, block)

    def score(step, buffer, chunk):
        pair = first_pair + step // blocks
        queries = diagonal(
            *(
                query_ref[block_rows(step), group_rows(2 * pair + member), :]
                .astype(jnp.float32)
                .reshape(side, HEAD_WIDTH)
                for member in range(2)
            )
        )
        keys = slice(chunk * chunk_keys, (chunk + 1) * chunk_keys)
        score_buf[buffer, :, keys] = contract(queries, prefix_ref[0, keys, pair_columns(pair)])

    def weigh(step, buffer, chunk):
        span = slice(chunk * chunk_rows, (chunk + 1) * chunk_rows)
        scores = score_buf[buffer, span, :]
        peak = jnp.max(scores, axis=1, keepdims=True)
        weights = jnp.exp2((scores - peak) * EXP2_SCALE)
        total = jnp.sum(weights, axis=1, keepdims=True)
        weight_buf[buffer, span, :] = weights.astype(jnp.bfloat16)
        inverse_buf[buffer, span, :] = jnp.broadcast_to(1.0 / total, (chunk_rows, LANES))
        lse = jnp.broadcast_to(peak * SCORE_SCALE + jnp.log(total), (chunk_rows, LANES))
        head = (first_pair + step // blocks) * 2 + chunk * chunk_rows // side
        slot = step % blocks * block + chunk * chunk_rows % side // GROUP
        lse_ref[slot, group_rows(head), :] = lse[:GROUP]
        lse_ref[slot + 1, group_rows(head), :] = lse[GROUP:]

    def gather_values(step, buffer):
        pair = first_pair + step // blocks
        accum = jnp.dot(
            weight_buf[buffer],
            prefix_ref[1, :, pair_columns(pair)],
            preferred_element_type=jnp.float32,
        )
        for member in range(2):
            span = slice(member * side, (member + 1) * side)
            normed = accum[span, columns_at(member)] * inverse_buf[buffer, span, :]
            out_ref[block_rows(step), group_rows(2 * pair + member), :] = normed.reshape(
                block, GROUP, HEAD_WIDTH
            )

    if steps <= UNROLLED_STEPS:
        for step in range(steps + 2):
            if beside and step == BESIDE_STEP:
                beside()
            for chunk in range(chunks):
                if step < steps and chunk % (chunks // score_chunks) == 0:
                    score(step, step % 2, chunk // (chunks // score_chunks))
                if 1 <= step <= steps:
                    weigh(step - 1, (step - 1) % 2, chunk)
            if step >= 2:
                gather_values(step - 2, step % 2)
    else:
        if beside:
            beside()

        def one_step(step, carry):
            for chunk in range(score_chunks):
                score(step, 0, chunk)
            for chunk in range(chunks):
                weigh(step, 0, chunk)
            gather_values(step, 0)
            return carry

        lax.fori_loop(0, steps, one_step, 0)


def attend_suffix(query, live, suffix_ref):
    suffix_length = suffix_ref.shape[2]
    pairs = range(KEY_VALUE_HEADS // 2)
    scores = jnp.concatenate(
        [
            contract(
                diagonal(query[group_rows(2 * pair)], query[group_rows(2 * pair + 1)]),
                suffix_ref[0, 0, :, pair_columns(pair)],
            )
            for pair in pairs
        ],
        axis=0,
    )
    scores = jnp.where(iota((1, suffix_length), 1) < live, scores, -jnp.inf)
    peak = jnp.max(scores, axis=1, keepdims=True)
    weights = jnp.exp2((scores - peak) * EXP2_SCALE)
    total = jnp.sum(weights, axis=1, keepdims=True)
    weights = weights.astype(jnp.bfloat16)
    accum = []
    for pair in pairs:
        both = jnp.dot(
            weights[2 * pair * GROUP : 2 * (pair + 1) * GROUP],
            suffix_ref[0, 1, :, pair_columns(pair)],
            preferred_element_type=jnp.float32,
        )
        accum += [both[:GROUP, :HEAD_WIDTH], both[GROUP:, HEAD_WIDTH:]]
    value = jnp.concatenate(accum, axis=0) * (1.0 / total)
    lse = peak * SCORE_SCALE + jnp.log(total)
    return value, jnp.broadcast_to(lse, (QUERY_HEADS, LANES))


def suffix_place(where_ref):
    places = where_ref[...].astype(jnp.float32)
    return jnp.sum(jnp.where(iota(places.shape, 1) == 0, places, 0.0)).astype(jnp.int32)


def far_kernel(
    where_ref,
    near_ref,
    far_ref,
    prefix_ref,
    suffix_ref,
    early_lse_ref,
    send_ref,
    part_ref,
    part_lse_ref,
    out_buf,
    lse_buf,
    *buffers,
):
    half = far_ref.shape[0]
    place = suffix_place(where_ref)
    is_far = place >= half
    near_row = jnp.minimum(place, half - 1)
    far_row = jnp.maximum(place - half, 0)
    near_query = near_ref[near_row].astype(jnp.float32)
    far_query = far_ref[far_row].astype(jnp.float32)
    query = jnp.where(is_far, far_query, near_query)

    def suffix():
        part_ref[...], part_lse_ref[...] = attend_suffix(query, where_ref[:, 1:2], suffix_ref)

    attend_prefix(far_ref, prefix_ref, out_buf, lse_buf, *buffers, beside=suffix)

    lse = part_lse_ref[...]
    out_buf[far_row], lse_buf[far_row] = merge_parts(
        [lse_buf[far_row], jnp.where(is_far, lse, -jnp.inf)], [out_buf[far_row], part_ref[...]]
    )
    part_lse_ref[...] = jnp.where(is_far, -jnp.inf, lse)

    def write(row):
        send_ref[row, :QUERY_HEADS] = out_buf[row].astype(jnp.bfloat16)
        send_ref[row, QUERY_HEADS:] = pack_lse(lse_buf[row])

    for_rows(half, write)


EARLY_PAIRS = KEY_VALUE_HEADS // 4
EARLY_HEADS = EARLY_PAIRS * 2 * GROUP


def near_kernel(near_ref, prefix_ref, out_ref, lse_ref, *buffers):
    attend_prefix(near_ref, prefix_ref, out_ref, lse_ref, *buffers, pairs=EARLY_PAIRS)


def rest_kernel(
    where_ref,
    near_ref,
    prefix_ref,
    part_ref,
    part_lse_ref,
    early_ref,
    early_lse_ref,
    keep_ref,
    keep_lse_ref,
    *buffers,
):
    row = jnp.minimum(suffix_place(where_ref), near_ref.shape[0] - 1)
    keep_ref[:, :EARLY_HEADS] = early_ref[...]
    keep_lse_ref[:, :EARLY_HEADS] = early_lse_ref[...]
    attend_prefix(
        near_ref,
        prefix_ref,
        keep_ref,
        keep_lse_ref,
        *buffers,
        first_pair=EARLY_PAIRS,
        pairs=KEY_VALUE_HEADS // 2 - EARLY_PAIRS,
    )
    keep_ref[row], keep_lse_ref[row] = merge_parts(
        [keep_lse_ref[row], part_lse_ref[...]], [keep_ref[row], part_ref[...]]
    )


def merge_parts(lses, values):
    highest = functools.reduce(jnp.maximum, lses)
    weights = [jnp.exp(lse - highest) for lse in lses]
    total = functools.reduce(jnp.add, weights)
    merged = functools.reduce(jnp.add, [w * value for w, value in zip(weights, values)])
    return merged * (1.0 / total), highest + jnp.log(total)


def fresh_kernel(query_ref, fresh_ref, keep_ref, keep_lse_ref, out_ref, out_lse_ref):
    key = spread_heads(fresh_ref[0, 0:1, :].astype(jnp.float32))
    value = spread_heads(fresh_ref[0, 1:2, :].astype(jnp.float32))
    products = query_ref[0].astype(jnp.float32) * key
    lse = jnp.sum(products, axis=1, keepdims=True) * SCORE_SCALE
    out_ref[0], out_lse_ref[0] = merge_parts([keep_lse_ref[0], lse], [keep_ref[0], value])


def merge_kernel(keep_ref, keep_lse_ref, *refs, rows, parts, landings):
    landed_refs, out_refs = refs[:landings], refs[landings:]
    size = rows // parts

    def merge(row):
        lses = [keep_lse_ref[row]] + [unpack_lse(ref[row, QUERY_HEADS:]) for ref in landed_refs]
        values = [keep_ref[row]] + [
            ref[row, :QUERY_HEADS].astype(jnp.float32) for ref in landed_refs
        ]
        return merge_parts(lses, values)

    if parts == 1:
        merged, _ = merge(0)
        for c in range(QUERY_HEADS):
            out_refs[0][:, columns_at(c)] = merged[c : c + 1].astype(jnp.bfloat16)
        return

    def keep(row):
        out_refs[0][row], out_refs[1][row] = merge(row)

    for_rows(size, keep)
    for i in range(1, parts):

        def send(row):
            merged, lse = merge(i * size + row)
            out_refs[1 + i][row, :QUERY_HEADS] = merged.astype(jnp.bfloat16)
            out_refs[1 + i][row, QUERY_HEADS:] = pack_lse(lse)

        for_rows(size, send)


def partial_shapes(rows):
    return (
        jax.ShapeDtypeStruct((rows, QUERY_HEADS, HEAD_WIDTH), jnp.float32),
        jax.ShapeDtypeStruct((rows, QUERY_HEADS, LANES), jnp.float32),
        jax.ShapeDtypeStruct((rows, BLOCK_ROWS, HEAD_WIDTH), jnp.bfloat16),
    )


def per_device(queries, prefix_key_value, suffix_key_value, fresh_key_value, lengths, home):
    slots = lax.axis_size("blk")
    bits = slots.bit_length() - 1
    assert queries.shape[0] == 1 and slots == 1 << bits and slots > 1
    vmem = pl.BlockSpec(memory_space=pltpu.VMEM)
    phases = exchange_phases(slots)

    def swap(array, step):
        return lax.ppermute(array, "blk", [(i, i ^ step) for i in range(slots)])

    def in_vmem(*arrays):
        return [pltpu.with_memory_space_constraint(array, pltpu.VMEM) for array in arrays]

    def join(kernel, rows, *arrays):
        return pl.pallas_call(
            kernel,
            out_shape=jax.ShapeDtypeStruct((rows, QUERY_HEADS, HEAD_WIDTH), jnp.bfloat16),
            in_specs=[vmem] * len(arrays),
            out_specs=vmem,
            compiler_params=pltpu.CompilerParams(vmem_limit_bytes=MERGE_VMEM),
            name="join",
        )(*in_vmem(*arrays))

    def exchange(arrays, distances):
        order = sorted(range(len(distances)), key=lambda i: distances[i])
        landed = {i: swap(arrays[i], distances[i]) for i in order}
        return [landed[i] for i in range(len(distances))]

    landed = swap(queries, phases[0][0])
    query, fresh, where = pl.pallas_call(
        functools.partial(stage_kernel, slots=slots),
        out_shape=(
            pltpu.VMEM((1, QUERY_HEADS, HEAD_WIDTH), jnp.bfloat16),
            pltpu.VMEM(fresh_key_value.shape, jnp.bfloat16),
            pltpu.VMEM((1, LANES), jnp.int32),
        ),
        in_specs=[pl.BlockSpec(memory_space=pltpu.HBM)] * 6,
        out_specs=(vmem,) * 3,
        scratch_shapes=[
            pltpu.VMEM((1, slots), jnp.int32),
            pltpu.VMEM((1, slots), jnp.int32),
            pltpu.VMEM(queries.shape, jnp.bfloat16),
            pltpu.SemaphoreType.DMA((4,)),
        ],
        compiler_params=pltpu.CompilerParams(vmem_limit_bytes=MERGE_VMEM),
        cost_estimate=pl.CostEstimate(flops=0, bytes_accessed=STAGE_BYTES, transcendentals=0),
        name="stage",
    )(
        *(
            pltpu.with_memory_space_constraint(array, pltpu.HBM)
            for array in (
                home.reshape(1, slots),
                lengths.reshape(1, slots),
                queries,
                fresh_key_value,
                prefix_key_value,
                suffix_key_value,
            )
        )
    )
    gathered = join(first_join_kernel, 2, query, landed)
    for phase in phases[1:-1]:
        landed = exchange([gathered] * len(partners(phase)), partners(phase))
        gathered = join(join_kernel, gathered.shape[0] << len(phase), gathered, *landed)

    half = slots // 2
    rows, prefix_length = step_rows(half), prefix_key_value.shape[1]
    shapes = partial_shapes(half)
    part_shape = jax.ShapeDtypeStruct((QUERY_HEADS, LANES), jnp.float32)
    early_shape = jax.ShapeDtypeStruct((half, EARLY_HEADS, LANES), jnp.float32)
    buffers = [
        pltpu.VMEM((2, rows, prefix_length), jnp.float32),
        pltpu.VMEM((2, rows, prefix_length), jnp.bfloat16),
        pltpu.VMEM((2, rows, LANES), jnp.float32),
    ]

    def attend(kernel, name, out_shape, scratch, *arrays):
        return pl.pallas_call(
            kernel,
            out_shape=out_shape,
            in_specs=[vmem] * len(arrays),
            out_specs=(vmem,) * len(out_shape),
            scratch_shapes=scratch + buffers,
            compiler_params=pltpu.CompilerParams(vmem_limit_bytes=ATTEND_VMEM),
            cost_estimate=pl.CostEstimate(
                flops=0, bytes_accessed=STAGE_BYTES // 4, transcendentals=0
            ),
            name=name,
        )(*in_vmem(*arrays))

    (other,) = exchange([gathered], phases[-1])
    early, early_lse = attend(
        near_kernel, "near", (early_shape, early_shape), [], gathered, prefix_key_value
    )
    send, part, part_lse = attend(
        far_kernel,
        "far",
        (shapes[2], part_shape, part_shape),
        [pltpu.VMEM(shape.shape, shape.dtype) for shape in shapes[:2]],
        where,
        gathered,
        other,
        prefix_key_value,
        suffix_key_value,
        early_lse,
    )
    (landed,) = exchange([send], phases[-1])
    keep, keep_lse = attend(
        rest_kernel,
        "rest",
        shapes[:2],
        [],
        where,
        gathered,
        prefix_key_value,
        part,
        part_lse,
        early,
        early_lse,
    )

    rows = half
    landed = [landed]
    for i, phase in enumerate(phases[::-1]):
        if i > 0:
            landed = exchange(sends, partners(phase))
        if i == len(phases) - 1:
            parts, shapes = 1, (jax.ShapeDtypeStruct((1, OUT_WIDTH), jnp.bfloat16),)
            keep, keep_lse = pl.pallas_call(
                fresh_kernel,
                out_shape=partial_shapes(1)[:2],
                in_specs=[vmem] * 4,
                out_specs=(vmem,) * 2,
                compiler_params=pltpu.CompilerParams(vmem_limit_bytes=MERGE_VMEM),
                cost_estimate=pl.CostEstimate(
                    flops=0, bytes_accessed=STAGE_BYTES // 8, transcendentals=0
                ),
                name="fresh",
            )(*in_vmem(query, fresh, keep, keep_lse))
        else:
            parts = 1 << len(phases[-2 - i])
            shapes = partial_shapes(rows // parts)
            shapes = shapes[:2] + shapes[2:] * (parts - 1)
        merged = pl.pallas_call(
            functools.partial(merge_kernel, rows=rows, parts=parts, landings=len(landed)),
            out_shape=shapes,
            in_specs=[vmem] * (2 + len(landed)),
            out_specs=(vmem,) * len(shapes),
            compiler_params=pltpu.CompilerParams(vmem_limit_bytes=MERGE_VMEM),
            name="merge",
        )(keep, keep_lse, *landed[::-1])
        if parts > 1:
            keep, keep_lse, *sends = merged
            rows = rows // parts
    return merged[0]


def solution(mesh):
    placed = (
        P(("groups", "blk"), None),
        P(None, ("groups", "blk"), None),
        P(("groups", "blk"), None, None, None),
        P(("groups", "blk"), None, None),
        P("groups"),
        P("groups"),
    )
    return jax.shard_map(
        per_device,
        mesh=mesh,
        in_specs=placed,
        out_specs=P(("groups", "blk"), None),
        check_vma=False,
    )
```

```python
import functools
import math

import jax
import jax.numpy as jnp
from jax import lax
from jax.experimental import pallas as pl
from jax.experimental.pallas import tpu as pltpu
from jax.sharding import PartitionSpec as P

QUERY_HEADS = 64
KEY_VALUE_HEADS = 8
HEAD_WIDTH = 128
LANES = 128
GROUP = QUERY_HEADS // KEY_VALUE_HEADS
OUT_WIDTH = QUERY_HEADS * HEAD_WIDTH

BLOCK_ROWS = QUERY_HEADS + 8

SCORE_SCALE = HEAD_WIDTH ** (-0.5)
EXP2_SCALE = SCORE_SCALE * math.log2(math.e)

STAGE_BYTES = 16 * 1024 * 1024
MERGE_VMEM = 16 * 1024 * 1024
ATTEND_VMEM = 44 * 1024 * 1024
UNROLLED_STEPS = 8
BESIDE_STEP = 4


def columns_at(head):
    if isinstance(head, int):
        return slice(head * HEAD_WIDTH, (head + 1) * HEAD_WIDTH)
    return pl.ds(pl.multiple_of(head * HEAD_WIDTH, HEAD_WIDTH), HEAD_WIDTH)


def iota(shape, dimension):
    return lax.broadcasted_iota(jnp.int32, shape, dimension)


def heads_down(row):
    sublane = iota((GROUP, HEAD_WIDTH), 0)
    tiles = []
    for head in range(KEY_VALUE_HEADS):
        tile = jnp.zeros((GROUP, HEAD_WIDTH), jnp.float32)
        for i in range(GROUP):
            tile = jnp.where(sublane == i, row[:, columns_at(head * GROUP + i)], tile)
        tiles.append(tile)
    return jnp.concatenate(tiles, axis=0)


def spread_heads(row):
    return jnp.concatenate(
        [
            jnp.broadcast_to(row[:, columns_at(head)], (GROUP, HEAD_WIDTH))
            for head in range(KEY_VALUE_HEADS)
        ],
        axis=0,
    )


def heads_along(values):
    shape = (QUERY_HEADS, LANES)
    own = (iota(shape, 1) & (QUERY_HEADS - 1)) == iota(shape, 0)
    return jnp.sum(jnp.where(own, values, 0.0), axis=0, keepdims=True)


def pack_lse(along):
    high = along.astype(jnp.bfloat16).astype(jnp.float32)
    rest = along - high
    middle = rest.astype(jnp.bfloat16).astype(jnp.float32)
    low = rest - middle
    tile = (8, LANES)
    first = jnp.where(iota(tile, 1) < QUERY_HEADS, high, middle)
    return jnp.where(iota(tile, 0) < 4, first, low).astype(jnp.bfloat16)


def unpack_lse(tile):
    tile = tile.astype(jnp.float32)
    first = tile[0:1]
    along = first + pltpu.roll(first, QUERY_HEADS, 1) + tile[4:5]
    shape = (QUERY_HEADS, LANES)
    chosen = jnp.where(iota(shape, 1) == iota(shape, 0), along, 0.0)
    return jnp.sum(chosen, axis=1, keepdims=True)


def exchange_phases(slots):
    steps = [(slots >> (i + 1)) | 1 for i in range(slots.bit_length() - 1)]
    phases = [[step] for step in steps]
    if len(steps) > 3:
        phases = phases[:-3] + [steps[-3:-1]] + phases[-1:]
    return phases


def partners(phase):
    return phase if len(phase) == 1 else [phase[0], phase[1], phase[0] | phase[1]]


def slot_of_row(rows, me, slots):
    distance = rows ^ me
    slot, other_core, place = 0, distance & 1, 0
    for phase in exchange_phases(slots)[:-1]:
        crossed = 0
        for step in phase:
            bit = lax.shift_right_logical(distance, step.bit_length() - 1) & 1
            slot = slot + bit * (1 << place)
            crossed = crossed | bit
            place += 1
        other_core = other_core ^ crossed
    return slot + other_core * (1 << place)


def for_rows(count, body):
    if count <= 16:
        for row in range(count):
            body(row)
    else:

        def one(row, carry):
            body(row)
            return carry

        lax.fori_loop(0, count, one, 0)


def stage_kernel(
    home_hbm, lengths_hbm, query_hbm, fresh_hbm, prefix_hbm, suffix_hbm,
    query_ref, fresh_ref, where_ref, home_buf, lengths_buf, query_buf, sems, *, slots
):
    pairs = (
        (home_hbm, home_buf),
        (lengths_hbm, lengths_buf),
        (query_hbm, query_buf),
        (fresh_hbm, fresh_ref),
    )
    copies = [
        pltpu.make_async_copy(source, target, sems.at[i])
        for i, (source, target) in enumerate(pairs)
    ]
    for copy in copies:
        copy.start()
    for copy in copies:
        copy.wait()
    me = lax.axis_index("blk")
    here = home_buf[...] == me
    row_ids = iota(here.shape, 1)

    def pick(values):
        chosen = jnp.where(here, values, 0).astype(jnp.float32)
        return jnp.sum(chosen, axis=1, keepdims=True).astype(jnp.int32)

    slot = pick(slot_of_row(row_ids, me, slots))
    where_ref[...] = jnp.where(iota(where_ref.shape, 1) == 0, slot, pick(lengths_buf[...]))
    query_ref[0] = heads_down(query_buf[...].astype(jnp.float32)).astype(jnp.bfloat16)


def first_join_kernel(query_ref, landed_ref, out_ref):
    out_ref[0] = query_ref[0]
    out_ref[1] = heads_down(landed_ref[...].astype(jnp.float32)).astype(jnp.bfloat16)


def join_kernel(*refs):
    rows = refs[0].shape[0]
    for i, ref in enumerate(refs[:-1]):
        refs[-1][i * rows : (i + 1) * rows] = ref[...]


def contract(left, right):
    return lax.dot_general(left, right, (((1,), (1,)), ((), ())), preferred_element_type=jnp.float32)


def pair_columns(pair):
    if isinstance(pair, int):
        return slice(pair * 2 * HEAD_WIDTH, (pair + 1) * 2 * HEAD_WIDTH)
    return pl.ds(pl.multiple_of(pair * 2 * HEAD_WIDTH, 2 * HEAD_WIDTH), 2 * HEAD_WIDTH)


def group_rows(head):
    if isinstance(head, int):
        return slice(head * GROUP, (head + 1) * GROUP)
    return pl.ds(pl.multiple_of(head * GROUP, GROUP), GROUP)


def diagonal(first, second):
    first = jnp.concatenate([first, jnp.zeros_like(first)], axis=1)
    second = jnp.concatenate([jnp.zeros_like(second), second], axis=1)
    return jnp.concatenate([first, second], axis=0).astype(jnp.bfloat16)


def step_rows(slots):
    return 2 * GROUP * min(slots, LANES // GROUP)


def attend_prefix(
    query_ref,
    prefix_ref,
    out_ref,
    lse_ref,
    score_buf,
    weight_buf,
    inverse_buf,
    first_pair=0,
    pairs=KEY_VALUE_HEADS // 2,
    beside=None,
):
    slots = query_ref.shape[0]
    rows = step_rows(slots)
    side = rows // 2
    block = side // GROUP
    blocks = slots // block
    steps = pairs * blocks
    prefix_length = prefix_ref.shape[1]
    chunk_rows = 2 * GROUP
    chunks = rows // chunk_rows
    score_chunks = 2
    chunk_keys = prefix_length // score_chunks

    def block_rows(step):
        start = step % blocks * block
        return slice(start, start + block) if isinstance(start, int) else pl.ds(start, block)

    def score(step, buffer, chunk):
        pair = first_pair + step // blocks
        queries = diagonal(
            *(
                query_ref[block_rows(step), group_rows(2 * pair + member), :]
                .astype(jnp.float32)
                .reshape(side, HEAD_WIDTH)
                for member in range(2)
            )
        )
        keys = slice(chunk * chunk_keys, (chunk + 1) * chunk_keys)
        score_buf[buffer, :, keys] = contract(queries, prefix_ref[0, keys, pair_columns(pair)])

    def weigh(step, buffer, chunk):
        span = slice(chunk * chunk_rows, (chunk + 1) * chunk_rows)
        scores = score_buf[buffer, span, :]
        peak = jnp.max(scores, axis=1, keepdims=True)
        weights = jnp.exp2((scores - peak) * EXP2_SCALE)
        total = jnp.sum(weights, axis=1, keepdims=True)
        weight_buf[buffer, span, :] = weights.astype(jnp.bfloat16)
        inverse_buf[buffer, span, :] = jnp.broadcast_to(1.0 / total, (chunk_rows, LANES))
        lse = jnp.broadcast_to(peak * SCORE_SCALE + jnp.log(total), (chunk_rows, LANES))
        head = (first_pair + step // blocks) * 2 + chunk * chunk_rows // side
        slot = step % blocks * block + chunk * chunk_rows % side // GROUP
        lse_ref[slot, group_rows(head), :] = lse[:GROUP]
        lse_ref[slot + 1, group_rows(head), :] = lse[GROUP:]

    def gather_values(step, buffer):
        pair = first_pair + step // blocks
        accum = jnp.dot(
            weight_buf[buffer],
            prefix_ref[1, :, pair_columns(pair)],
            preferred_element_type=jnp.float32,
        )
        for member in range(2):
            span = slice(member * side, (member + 1) * side)
            normed = accum[span, columns_at(member)] * inverse_buf[buffer, span, :]
            out_ref[block_rows(step), group_rows(2 * pair + member), :] = normed.reshape(
                block, GROUP, HEAD_WIDTH
            )

    if steps <= UNROLLED_STEPS:
        for step in range(steps + 2):
            if beside and step == BESIDE_STEP:
                beside()
            for chunk in range(chunks):
                if step < steps and chunk % (chunks // score_chunks) == 0:
                    score(step, step % 2, chunk // (chunks // score_chunks))
                if 1 <= step <= steps:
                    weigh(step - 1, (step - 1) % 2, chunk)
            if step >= 2:
                gather_values(step - 2, step % 2)
    else:
        if beside:
            beside()

        def one_step(step, carry):
            for chunk in range(score_chunks):
                score(step, 0, chunk)
            for chunk in range(chunks):
                weigh(step, 0, chunk)
            gather_values(step, 0)
            return carry

        lax.fori_loop(0, steps, one_step, 0)


def attend_suffix(query, live, suffix_ref):
    suffix_length = suffix_ref.shape[2]
    pairs = range(KEY_VALUE_HEADS // 2)
    scores = jnp.concatenate(
        [
            contract(
                diagonal(query[group_rows(2 * pair)], query[group_rows(2 * pair + 1)]),
                suffix_ref[0, 0, :, pair_columns(pair)],
            )
            for pair in pairs
        ],
        axis=0,
    )
    scores = jnp.where(iota((1, suffix_length), 1) < live, scores, -jnp.inf)
    peak = jnp.max(scores, axis=1, keepdims=True)
    weights = jnp.exp2((scores - peak) * EXP2_SCALE)
    total = jnp.sum(weights, axis=1, keepdims=True)
    weights = weights.astype(jnp.bfloat16)
    accum = []
    for pair in pairs:
        both = jnp.dot(
            weights[2 * pair * GROUP : 2 * (pair + 1) * GROUP],
            suffix_ref[0, 1, :, pair_columns(pair)],
            preferred_element_type=jnp.float32,
        )
        accum += [both[:GROUP, :HEAD_WIDTH], both[GROUP:, HEAD_WIDTH:]]
    value = jnp.concatenate(accum, axis=0) * (1.0 / total)
    lse = peak * SCORE_SCALE + jnp.log(total)
    return value, jnp.broadcast_to(lse, (QUERY_HEADS, LANES))


def suffix_place(where_ref):
    places = where_ref[...].astype(jnp.float32)
    return jnp.sum(jnp.where(iota(places.shape, 1) == 0, places, 0.0)).astype(jnp.int32)


def far_kernel(
    where_ref,
    near_ref,
    far_ref,
    prefix_ref,
    suffix_ref,
    early_lse_ref,
    send_ref,
    part_ref,
    part_lse_ref,
    out_buf,
    lse_buf,
    *buffers,
):
    half = far_ref.shape[0]
    place = suffix_place(where_ref)
    is_far = place >= half
    near_row = jnp.minimum(place, half - 1)
    far_row = jnp.maximum(place - half, 0)
    near_query = near_ref[near_row].astype(jnp.float32)
    far_query = far_ref[far_row].astype(jnp.float32)
    query = jnp.where(is_far, far_query, near_query)

    def suffix():
        part_ref[...], part_lse_ref[...] = attend_suffix(query, where_ref[:, 1:2], suffix_ref)

    attend_prefix(far_ref, prefix_ref, out_buf, lse_buf, *buffers, beside=suffix)

    lse = part_lse_ref[...]
    out_buf[far_row], lse_buf[far_row] = merge_whole(
        [lse_buf[far_row], jnp.where(is_far, lse, -jnp.inf)], [out_buf[far_row], part_ref[...]]
    )
    part_lse_ref[...] = jnp.where(is_far, -jnp.inf, lse)

    def write(row):
        send_ref[row, :QUERY_HEADS] = out_buf[row].astype(jnp.bfloat16)
        send_ref[row, QUERY_HEADS:] = pack_lse(heads_along(lse_buf[row]))

    for_rows(half, write)


EARLY_PAIRS = KEY_VALUE_HEADS // 4
EARLY_HEADS = EARLY_PAIRS * 2 * GROUP


def near_kernel(near_ref, prefix_ref, out_ref, lse_ref, *buffers):
    attend_prefix(near_ref, prefix_ref, out_ref, lse_ref, *buffers, pairs=EARLY_PAIRS)


def rest_kernel(
    where_ref,
    near_ref,
    prefix_ref,
    part_ref,
    part_lse_ref,
    early_ref,
    early_lse_ref,
    keep_ref,
    keep_lse_ref,
    *buffers,
):
    row = jnp.minimum(suffix_place(where_ref), near_ref.shape[0] - 1)
    keep_ref[:, :EARLY_HEADS] = early_ref[...]
    keep_lse_ref[:, :EARLY_HEADS] = early_lse_ref[...]
    attend_prefix(
        near_ref,
        prefix_ref,
        keep_ref,
        keep_lse_ref,
        *buffers,
        first_pair=EARLY_PAIRS,
        pairs=KEY_VALUE_HEADS // 2 - EARLY_PAIRS,
    )
    keep_ref[row], keep_lse_ref[row] = merge_whole(
        [keep_lse_ref[row], part_lse_ref[...]], [keep_ref[row], part_ref[...]]
    )


def merge_parts(lses, values):
    highest = functools.reduce(jnp.maximum, lses)
    weights = [jnp.exp(lse - highest) for lse in lses]
    total = functools.reduce(jnp.add, weights)
    merged = functools.reduce(jnp.add, [w * value for w, value in zip(weights, values)])
    return merged * (1.0 / total), highest, total


def merge_whole(lses, values):
    merged, highest, total = merge_parts(lses, values)
    return merged, highest + jnp.log(total)


def fresh_kernel(query_ref, fresh_ref, keep_ref, keep_lse_ref, out_ref, out_lse_ref):
    key = spread_heads(fresh_ref[0, 0:1, :].astype(jnp.float32))
    value = spread_heads(fresh_ref[0, 1:2, :].astype(jnp.float32))
    products = query_ref[0].astype(jnp.float32) * key
    lse = jnp.sum(products, axis=1, keepdims=True) * SCORE_SCALE
    out_ref[0], out_lse_ref[0] = merge_whole([keep_lse_ref[0], lse], [keep_ref[0], value])


def merge_kernel(keep_ref, keep_lse_ref, *refs, rows, parts, landings):
    landed_refs, out_refs = refs[:landings], refs[landings:]
    size = rows // parts

    def merge(row):
        lses = [keep_lse_ref[row]] + [unpack_lse(ref[row, QUERY_HEADS:]) for ref in landed_refs]
        values = [keep_ref[row]] + [
            ref[row, :QUERY_HEADS].astype(jnp.float32) for ref in landed_refs
        ]
        return merge_parts(lses, values)

    if parts == 1:
        merged, _, _ = merge(0)
        for c in range(QUERY_HEADS):
            out_refs[0][:, columns_at(c)] = merged[c : c + 1].astype(jnp.bfloat16)
        return

    def keep(row):
        out_refs[0][row], highest, total = merge(row)
        out_refs[1][row] = highest + jnp.log(total)

    for_rows(size, keep)
    for i in range(1, parts):

        def send(row):
            merged, highest, total = merge(i * size + row)
            lse = heads_along(highest) + jnp.log(heads_along(total))
            out_refs[1 + i][row, :QUERY_HEADS] = merged.astype(jnp.bfloat16)
            out_refs[1 + i][row, QUERY_HEADS:] = pack_lse(lse)

        for_rows(size, send)


def partial_shapes(rows):
    return (
        jax.ShapeDtypeStruct((rows, QUERY_HEADS, HEAD_WIDTH), jnp.float32),
        jax.ShapeDtypeStruct((rows, QUERY_HEADS, LANES), jnp.float32),
        jax.ShapeDtypeStruct((rows, BLOCK_ROWS, HEAD_WIDTH), jnp.bfloat16),
    )


def per_device(queries, prefix_key_value, suffix_key_value, fresh_key_value, lengths, home):
    slots = lax.axis_size("blk")
    bits = slots.bit_length() - 1
    assert queries.shape[0] == 1 and slots == 1 << bits and slots > 1
    vmem = pl.BlockSpec(memory_space=pltpu.VMEM)
    phases = exchange_phases(slots)

    def swap(array, step):
        return lax.ppermute(array, "blk", [(i, i ^ step) for i in range(slots)])

    def in_vmem(*arrays):
        return [pltpu.with_memory_space_constraint(array, pltpu.VMEM) for array in arrays]

    def join(kernel, rows, *arrays):
        return pl.pallas_call(
            kernel,
            out_shape=jax.ShapeDtypeStruct((rows, QUERY_HEADS, HEAD_WIDTH), jnp.bfloat16),
            in_specs=[vmem] * len(arrays),
            out_specs=vmem,
            compiler_params=pltpu.CompilerParams(vmem_limit_bytes=MERGE_VMEM),
            name="join",
        )(*in_vmem(*arrays))

    def exchange(arrays, distances):
        order = sorted(range(len(distances)), key=lambda i: distances[i])
        landed = {i: swap(arrays[i], distances[i]) for i in order}
        return [landed[i] for i in range(len(distances))]

    landed = swap(queries, phases[0][0])
    query, fresh, where = pl.pallas_call(
        functools.partial(stage_kernel, slots=slots),
        out_shape=(
            pltpu.VMEM((1, QUERY_HEADS, HEAD_WIDTH), jnp.bfloat16),
            pltpu.VMEM(fresh_key_value.shape, jnp.bfloat16),
            pltpu.VMEM((1, LANES), jnp.int32),
        ),
        in_specs=[pl.BlockSpec(memory_space=pltpu.HBM)] * 6,
        out_specs=(vmem,) * 3,
        scratch_shapes=[
            pltpu.VMEM((1, slots), jnp.int32),
            pltpu.VMEM((1, slots), jnp.int32),
            pltpu.VMEM(queries.shape, jnp.bfloat16),
            pltpu.SemaphoreType.DMA((4,)),
        ],
        compiler_params=pltpu.CompilerParams(vmem_limit_bytes=MERGE_VMEM),
        cost_estimate=pl.CostEstimate(flops=0, bytes_accessed=STAGE_BYTES, transcendentals=0),
        name="stage",
    )(
        *(
            pltpu.with_memory_space_constraint(array, pltpu.HBM)
            for array in (
                home.reshape(1, slots),
                lengths.reshape(1, slots),
                queries,
                fresh_key_value,
                prefix_key_value,
                suffix_key_value,
            )
        )
    )
    gathered = join(first_join_kernel, 2, query, landed)
    for phase in phases[1:-1]:
        landed = exchange([gathered] * len(partners(phase)), partners(phase))
        gathered = join(join_kernel, gathered.shape[0] << len(phase), gathered, *landed)

    half = slots // 2
    rows, prefix_length = step_rows(half), prefix_key_value.shape[1]
    shapes = partial_shapes(half)
    part_shape = jax.ShapeDtypeStruct((QUERY_HEADS, LANES), jnp.float32)
    early_shape = jax.ShapeDtypeStruct((half, EARLY_HEADS, LANES), jnp.float32)
    buffers = [
        pltpu.VMEM((2, rows, prefix_length), jnp.float32),
        pltpu.VMEM((2, rows, prefix_length), jnp.bfloat16),
        pltpu.VMEM((2, rows, LANES), jnp.float32),
    ]

    def attend(kernel, name, out_shape, scratch, *arrays):
        return pl.pallas_call(
            kernel,
            out_shape=out_shape,
            in_specs=[vmem] * len(arrays),
            out_specs=(vmem,) * len(out_shape),
            scratch_shapes=scratch + buffers,
            compiler_params=pltpu.CompilerParams(vmem_limit_bytes=ATTEND_VMEM),
            cost_estimate=pl.CostEstimate(
                flops=0, bytes_accessed=STAGE_BYTES // 4, transcendentals=0
            ),
            name=name,
        )(*in_vmem(*arrays))

    (other,) = exchange([gathered], phases[-1])
    early, early_lse = attend(
        near_kernel, "near", (early_shape, early_shape), [], gathered, prefix_key_value
    )
    send, part, part_lse = attend(
        far_kernel,
        "far",
        (shapes[2], part_shape, part_shape),
        [pltpu.VMEM(shape.shape, shape.dtype) for shape in shapes[:2]],
        where,
        gathered,
        other,
        prefix_key_value,
        suffix_key_value,
        early_lse,
    )
    (landed,) = exchange([send], phases[-1])
    keep, keep_lse = attend(
        rest_kernel,
        "rest",
        shapes[:2],
        [],
        where,
        gathered,
        prefix_key_value,
        part,
        part_lse,
        early,
        early_lse,
    )

    rows = half
    landed = [landed]
    for i, phase in enumerate(phases[::-1]):
        if i > 0:
            landed = exchange(sends, partners(phase))
        if i == len(phases) - 1:
            parts, shapes = 1, (jax.ShapeDtypeStruct((1, OUT_WIDTH), jnp.bfloat16),)
            keep, keep_lse = pl.pallas_call(
                fresh_kernel,
                out_shape=partial_shapes(1)[:2],
                in_specs=[vmem] * 4,
                out_specs=(vmem,) * 2,
                compiler_params=pltpu.CompilerParams(vmem_limit_bytes=MERGE_VMEM),
                cost_estimate=pl.CostEstimate(
                    flops=0, bytes_accessed=STAGE_BYTES // 8, transcendentals=0
                ),
                name="fresh",
            )(*in_vmem(query, fresh, keep, keep_lse))
        else:
            parts = 1 << len(phases[-2 - i])
            shapes = partial_shapes(rows // parts)
            shapes = shapes[:2] + shapes[2:] * (parts - 1)
        merged = pl.pallas_call(
            functools.partial(merge_kernel, rows=rows, parts=parts, landings=len(landed)),
            out_shape=shapes,
            in_specs=[vmem] * (2 + len(landed)),
            out_specs=(vmem,) * len(shapes),
            compiler_params=pltpu.CompilerParams(vmem_limit_bytes=MERGE_VMEM),
            name="merge",
        )(keep, keep_lse, *landed[::-1])
        if parts > 1:
            keep, keep_lse, *sends = merged
            rows = rows // parts
    return merged[0]


def solution(mesh):
    placed = (
        P(("groups", "blk"), None),
        P(None, ("groups", "blk"), None),
        P(("groups", "blk"), None, None, None),
        P(("groups", "blk"), None, None),
        P("groups"),
        P("groups"),
    )
    return jax.shard_map(
        per_device,
        mesh=mesh,
        in_specs=placed,
        out_specs=P(("groups", "blk"), None),
        check_vma=False,
    )
```
